32 devices in a mesh: region: 8 (over z, core), head: 4 (over y, x).
Axes of the slice: x: 2, y: 2, z: 4, core: 2. Of those that a mesh axis runs over, the one named last changes fastest.
Arguments:
- fine_tokens: float32 [18432, 512], P(('region', 'head')), may hold values from -6 to 6
- fine_shift: int32 [1], replicated, may hold values from 1 to 143
- window_counts: int32 [32], P('region'), may hold values from 36 to 144
- fine_qkv: bfloat16 [512, 1536], replicated, may hold values from -4 to 4
- fine_proj: bfloat16 [512, 512], replicated, may hold values from -0.25 to 0.25
- fine_up: bfloat16 [512, 2048], replicated, may hold values from -0.25 to 0.25
- fine_down: bfloat16 [2048, 512], replicated, may hold values from -0.125 to 0.125
- merge_weight: bfloat16 [2048, 1024], replicated, may hold values from -0.125 to 0.125
- coarse_qkv: bfloat16 [1024, 3072], P('region', 'head'), may hold values from -4 to 4
- coarse_proj: bfloat16 [1024, 1024], P('head', 'region'), may hold values from -0.1875 to 0.1875
- coarse_up: bfloat16 [1024, 4096], P('region', 'head'), may hold values from -0.1875 to 0.1875
- coarse_down: bfloat16 [4096, 1024], P('head', 'region'), may hold values from -0.09375 to 0.09375
- expand_weight: bfloat16 [1024, 2048], replicated, may hold values from -0.1875 to 0.1875
- out_weight: bfloat16 [1024, 512], replicated, may hold values from -0.1875 to 0.1875
Outputs:
- fine_result: float32 [18432, 512], P(('region', 'head'))
The draws below stay inside these ranges and needn't reach their ends.
All inputs are finite; a program needn't handle non-finite values.
Results may differ from the reference program's by a relative error of at most 0.012.
Values may be sent and summed in bfloat16 or wider, within the bound.
A program may use at most 128 MiB of HBM per device.

```python
import jax
import jax.numpy as jnp
from jax import lax

C = 512
HD = 64
HF = 8
D2 = 1024
HC = 16
FFF = 2048
FFC = 4096
WIN = 144
NTOK = 18432
NCW = 32


def drawn_qkv(key, channels, head_count):
    base = jax.random.normal(jax.random.fold_in(key, 11), (channels, head_count, 3, HD), jnp.float32)
    base = jnp.clip(base, -4.0, 4.0) * channels ** (-0.5)
    base = jnp.clip(base, -4.0, 4.0)
    return base.reshape(channels, head_count * 3 * HD)


def draw_fine_qkv(key, part):
    return drawn_qkv(key, C, HF).astype(jnp.bfloat16)


def draw_coarse_qkv(key, part):
    return drawn_qkv(key, D2, HC).astype(jnp.bfloat16)


def place_ends(entries, key, smallest, top_value):
    spot = [jax.random.randint(jax.random.fold_in(key, axis), (), 0, length) for axis, length in enumerate(entries.shape)]
    widest = entries.shape.index(max(entries.shape))
    neighbour = spot[:widest] + [(spot[widest] + 1) % entries.shape[widest]] + spot[widest + 1:]
    return entries.at[tuple(spot)].set(smallest).at[tuple(neighbour)].set(top_value)


def levels(own_key, shape, shards, least, top_value):
    loudness = 1.0
    for axis_at, shards_of in shards:
        steps = jax.random.uniform(jax.random.fold_in(jax.random.fold_in(own_key, 6), axis_at), (shards_of,), jnp.float32, least / len(shards), top_value / len(shards))
        loudness = loudness * jnp.repeat(jnp.exp(steps), shape[axis_at] // shards_of).reshape((-1,) + (1,) * (len(shape) - 1 - axis_at))
    return loudness


def normal_values(key, shape, deviation, limit, cuts=(), kind=jnp.bfloat16):
    drawn = jax.random.normal(key, shape, jnp.float32) * deviation
    if len(cuts) > 0:
        drawn = levels(key, shape, cuts, -0.22, 0.18) * drawn
    return jnp.clip(drawn, min=-limit, max=limit).astype(kind)


def setup_inputs(seed: int = 0) -> dict:
    keys = jax.random.split(jax.random.key(seed), 15)
    fine_tokens = normal_values(keys[0], (NTOK, C), 1.0, 6.0, ((0, 32),), jnp.float32)
    fine_shift = jax.random.randint(keys[1], (1,), 1, WIN).astype(jnp.int32)
    window_counts = place_ends(jax.random.randint(keys[2], (NCW,), WIN // 4, WIN + 1), jax.random.fold_in(keys[2], 1), WIN // 4, WIN).astype(jnp.int32)
    fine_qkv = draw_fine_qkv(jax.random.fold_in(keys[14], 71), 0)
    fine_proj = normal_values(keys[4], (C, C), C ** -0.5, 0.25)
    fine_up = normal_values(keys[5], (C, FFF), C ** -0.5, 0.25)
    fine_down = normal_values(keys[6], (FFF, C), FFF ** -0.5, 0.125)
    merge_weight = normal_values(keys[7], (4 * C, D2), (4 * C) ** -0.5, 0.125)
    coarse_qkv = draw_coarse_qkv(jax.random.fold_in(keys[14], 71), 0)
    coarse_proj = normal_values(keys[9], (D2, D2), D2 ** -0.5, 0.1875, ((0, 4), (1, 8)))
    coarse_up = normal_values(keys[10], (D2, FFC), D2 ** -0.5, 0.1875, ((0, 8), (1, 4)))
    coarse_down = normal_values(keys[11], (FFC, D2), FFC ** -0.5, 0.09375, ((0, 4), (1, 8)))
    expand_weight = normal_values(keys[12], (D2, 4 * C), D2 ** -0.5, 0.1875)
    out_weight = normal_values(keys[13], (2 * C, C), (2 * C) ** -0.5, 0.1875)
    return dict(fine_tokens=fine_tokens, fine_shift=fine_shift, window_counts=window_counts, fine_qkv=fine_qkv, fine_proj=fine_proj, fine_up=fine_up, fine_down=fine_down, merge_weight=merge_weight, coarse_qkv=coarse_qkv, coarse_proj=coarse_proj, coarse_up=coarse_up, coarse_down=coarse_down, expand_weight=expand_weight, out_weight=out_weight)


def layer_norm(values):
    average = lax.optimization_barrier(jnp.mean(values, axis=-1, keepdims=True))
    centred = values - average
    spread = lax.optimization_barrier(jnp.mean(centred * centred, axis=-1, keepdims=True))
    return centred * lax.rsqrt(spread + 1e-05)

def window_attention(normed, qkv_weight, proj_weight, head_count, head_size, window, counts):
    row_count = normed.shape[0]
    packed = jnp.dot(normed, qkv_weight, preferred_element_type=jnp.float32).astype(jnp.bfloat16)
    packed = lax.optimization_barrier(packed)
    packed = packed.reshape(row_count // window, window, head_count, 3, head_size).astype(jnp.float32)
    queries = packed[:, :, :, 0]
    key_part = packed[:, :, :, 1]
    value_part = packed[:, :, :, 2]
    scores = jnp.einsum('wqhd,wkhd->whqk', queries, key_part) * head_size ** (-0.5)
    if counts is not None:
        position = jnp.arange(window, dtype=jnp.int32)
        visible = position[None, :] < counts[:, None]
        scores = jnp.where(visible[:, None, None, :], scores, -1e+30)
    row_max = lax.optimization_barrier(jnp.max(scores, axis=-1, keepdims=True))
    raised = jnp.exp(scores - row_max)
    weights = (raised / lax.optimization_barrier(jnp.sum(raised, axis=-1, keepdims=True))).astype(jnp.bfloat16)
    weights = lax.optimization_barrier(weights).astype(jnp.float32)
    blended = jnp.einsum('whqk,wkhd->wqhd', weights, value_part).astype(jnp.bfloat16)
    blended = blended.reshape(row_count, head_count * head_size)
    return jnp.dot(blended, proj_weight, preferred_element_type=jnp.float32)

def feed_forward(normed, up_weight, down_weight):
    hidden = jnp.dot(normed, up_weight, preferred_element_type=jnp.float32)
    hidden = jax.nn.gelu(hidden, approximate=False).astype(jnp.bfloat16)
    return jnp.dot(hidden, down_weight, preferred_element_type=jnp.float32)

def reference(fine_tokens, fine_shift, window_counts, fine_qkv, fine_proj, fine_up, fine_down, merge_weight, coarse_qkv, coarse_proj, coarse_up, coarse_down, expand_weight, out_weight):
    offset = fine_shift[0]
    normed = layer_norm(fine_tokens).astype(jnp.bfloat16)
    rolled = jnp.roll(normed, -offset, axis=0)
    attended = window_attention(rolled, fine_qkv, fine_proj, HF, HD, WIN, None)
    fine_mid = fine_tokens + jnp.roll(attended, offset, axis=0)
    fine_out = fine_mid + feed_forward(layer_norm(fine_mid).astype(jnp.bfloat16), fine_up, fine_down)
    merged = fine_out.reshape(fine_out.shape[0] // 4, 4 * fine_out.shape[1])
    grouped = layer_norm(merged).astype(jnp.bfloat16)
    coarse = jnp.dot(grouped, merge_weight, preferred_element_type=jnp.float32)
    coarse_norm = layer_norm(coarse).astype(jnp.bfloat16)
    coarse_mid = coarse + window_attention(coarse_norm, coarse_qkv, coarse_proj, HC, HD, WIN, window_counts)
    coarse_out = coarse_mid + feed_forward(layer_norm(coarse_mid).astype(jnp.bfloat16), coarse_up, coarse_down)
    expanded = jnp.dot(coarse_out.astype(jnp.bfloat16), expand_weight, preferred_element_type=jnp.float32).astype(jnp.bfloat16)
    spread_rows = expanded.reshape(fine_out.shape[0], fine_out.shape[1])
    joined = jnp.concatenate([fine_out.astype(jnp.bfloat16), spread_rows], axis=1)
    return jnp.dot(joined, out_weight, preferred_element_type=jnp.float32)
```

```python
import functools

import jax
import jax.numpy as jnp
from jax import lax
from jax.experimental import pallas as pl
from jax.experimental.pallas import tpu as pltpu
from jax.sharding import PartitionSpec as P

C = 512
HD = 64
HF = 8
WIN = 144
HEADS = HF
MESH = pl.DeviceIdType.MESH
F32 = jnp.float32
BF16 = jnp.bfloat16


def norm(values):
    average = jnp.mean(values, axis=-1, keepdims=True)
    centred = values - average
    spread = jnp.mean(centred * centred, axis=-1, keepdims=True)
    return centred * lax.rsqrt(spread + 1e-05)


def gelu(values):
    return 0.5 * values * (1.0 + lax.erf(values * (0.5**0.5)))


def dot(left, right):
    return jnp.dot(left, right, preferred_element_type=F32)


def flip(index, mask):
    result = index
    bit = 1
    while bit <= mask:
        if mask & bit:
            result = result + (1 - 2 * ((index // bit) % 2)) * bit
        bit *= 2
    return result


def attend(packed, head_count, count):
    blended = []
    for head in range(head_count):
        base = head * 3 * HD
        query = packed[:, base : base + HD]
        key = packed[:, base + HD : base + 2 * HD]
        value = packed[:, base + 2 * HD : base + 3 * HD]
        scores = lax.dot_general(
            query, key, (((1,), (1,)), ((), ())), preferred_element_type=F32
        ) * (HD**-0.5)
        if count is not None:
            place = lax.broadcasted_iota(jnp.int32, scores.shape, 1)
            scores = jnp.where(place < count, scores, -1e30)
        raised = jnp.exp(scores - jnp.max(scores, axis=-1, keepdims=True))
        weights = (raised / jnp.sum(raised, axis=-1, keepdims=True)).astype(BF16)
        blended.append(dot(weights, value).astype(BF16))
    return blended


def kernel(
    region_count, head_count,
    shift, counts, tokens, w_qkv, w_proj, w_up, w_down, w_merge,
    c_qkv, c_proj, c_up, c_down, w_expand, w_out,
    out,
    v_qkv, v_proj, v_up, v_down, v_merge, v_expand, v_out,
    g_qkv, g_proj, g_up, g_down,
    extended, rolled, packed, blended, fine, fine_bf, hidden, grouped,
    coarse, shared, c_packed, sent_blend, got_blend, mid, c_normed, c_hidden, term, parts, got_parts,
    wide, spread, lanes,
    local_sem, halo_send, halo_recv, own_sem, z_send, w_recv, p_send, q_send, q_recv, x_send, x_recv,
    a_send, a_recv, b_send, b_recv, m_send, m_recv, r_send, r_recv,
):
    region, head = lax.axis_index("region"), lax.axis_index("head")
    chips = region_count // 2
    chip, core = region // 2, region % 2
    rows = tokens.shape[0]
    blocks = rows // WIN
    flat = region * head_count + head
    total = region_count * head_count
    before, after = (flat + total - 1) % total, (flat + 1) % total
    before = (before // head_count, before % head_count)
    after = (after // head_count, after % head_count)
    partner = (chip * 2 + 1 - core, head)
    plane = [(region, flip(head, k)) for k in range(head_count)]
    ways = (1, -1)

    def line(way):
        return (((chip + way + chips) % chips) * 2 + core, head)

    barrier = pltpu.get_barrier_semaphore()
    greeted = [before, after, partner, line(1), line(-1)] + plane[1:]
    for device in greeted:
        pl.semaphore_signal(barrier, inc=1, device_id=device, device_id_type=MESH)

    QKV, PROJ, UP0, UP1, DOWN = range(5)
    half_up = c_up.shape[0] // 2
    shards = [c_qkv, c_proj, c_up.at[pl.ds(0, half_up)], c_up.at[pl.ds(half_up, half_up)], c_down]

    def slot(which, owner):
        if which == QKV:
            return g_qkv.at[pl.ds(owner * c_qkv.shape[0], c_qkv.shape[0])]
        if which == PROJ:
            return g_proj.at[head, owner]
        if which == UP0:
            return g_up.at[pl.ds(owner * c_up.shape[0], half_up)]
        if which == UP1:
            return g_up.at[pl.ds(owner * c_up.shape[0] + half_up, half_up)]
        return g_down.at[owner]

    own_shards = []
    for which in range(5):
        own_shards.append(pltpu.make_async_copy(shards[which], slot(which, region), own_sem.at[which]))
    own = []
    for at, (source, target) in enumerate(
        [(w_qkv, v_qkv), (w_proj, v_proj), (w_up, v_up), (w_down, v_down), (w_merge, v_merge),
         (w_expand, v_expand), (w_out, v_out)]
    ):
        own.append(pltpu.make_async_copy(source, target, local_sem.at[at]))
    own[0].start()
    for copy in own_shards + own[1:]:
        copy.start()

    def remote(source, target, send, recv, device):
        return pltpu.make_async_remote_copy(
            src_ref=source, dst_ref=target, send_sem=send, recv_sem=recv,
            device_id=device, device_id_type=MESH,
        )

    extended[WIN : WIN + rows, :] = norm(tokens[...]).astype(BF16)
    pl.semaphore_wait(barrier, len(greeted))

    halo_left = remote(extended.at[pl.ds(WIN, WIN)], extended.at[pl.ds(WIN + rows, WIN)],
                       halo_send.at[0], halo_recv.at[0], before)
    halo_right = remote(extended.at[pl.ds(rows, WIN)], extended.at[pl.ds(0, WIN)],
                        halo_send.at[1], halo_recv.at[1], after)
    halo_left.start()
    halo_right.start()

    def came(way, far):
        return (chip - way * far >= 0) & (chip - way * far < chips)

    def goes(way):
        return (chip + way >= 0) & (chip + way < chips)

    def owner_of(way, far):
        return ((chip - way * far + chips * chips) % chips) * 2 + core

    def hop(which, way, far):
        owner = owner_of(way, far)
        place = slot(which, owner)
        return remote(shards[which] if far == 0 else place, place,
                      z_send.at[which, (way < 0) * chips + far], w_recv.at[which, owner], line(way))

    def pass_over(which, owner, source=None):
        place = slot(which, owner)
        return remote(place if source is None else source, place, p_send.at[which, owner // 2], w_recv.at[which, owner], partner)

    def spread_proj(owner, at, source=None):
        for k in range(1, head_count):
            piece = g_proj.at[head, owner]
            remote(piece if source is None else source, piece, q_send.at[k, at], q_recv.at[k, owner // 2], plane[k]).start()

    def send_own(which):
        for way in ways:
            @pl.when(goes(way))
            def _():
                hop(which, way, 0).start()

    def arrive(which, way, far, forward):
        owner = owner_of(way, far)
        remote(slot(which, owner), slot(which, owner), p_send.at[which, owner // 2],
               w_recv.at[which, owner], line(way)).wait_recv()
        if forward:
            hop(which, way, far).start()
        pass_over(which, owner).start()
        if which == PROJ:
            spread_proj(owner, owner // 2)

    def forward(which, far):
        if far > chips - 2:
            return
        for way in ways:
            @pl.when(came(way, far) & goes(way))
            def _():
                arrive(which, way, far, True)

    def collect(which, fars):
        for far in fars:
            for way in ways:
                @pl.when(came(way, far) & jnp.logical_not(goes(way)))
                def _():
                    arrive(which, way, far, False)

    def take_one(which, owner):
        remote(slot(which, owner), slot(which, owner), p_send.at[which, owner // 2],
               w_recv.at[which, owner], partner).wait_recv()

    def take_over(which):
        for s in range(chips):
            take_one(which, ((chip + s) % chips) * 2 + 1 - core)

    fars = range(1, chips)

    for which in (PROJ, QKV, UP0):
        send_own(which)
    spread_proj(region, chip, shards[PROJ])
    for which in (PROJ, QKV, UP0, UP1, DOWN):
        pass_over(which, region, shards[which]).start()

    relay = head_count == 4

    def half_of(piece_of, h, i):
        whole = piece_of(h)
        half = whole.shape[1] // 2
        return whole.at[:, pl.ds(i * half, half)]

    def half_copy(piece_of, h, k, i, send, recv):
        piece = half_of(piece_of, h, i)
        return remote(piece, piece, send.at[k, i], recv.at[k, i], plane[k])

    def gather(piece_of, send, recv):
        copies = []
        for i in range(2):
            for k in range(1, 3 if relay else head_count):
                copy = half_copy(piece_of, head, k, i if k != 2 else 1 - i, send, recv)
                copy.start()
                copies.append(copy)
        return copies

    def far_half(piece_of, mask, i, send, recv, device):
        piece = half_of(piece_of, flip(head, mask), i)
        return remote(piece, piece, send.at[3, i], recv.at[3, i], device)

    def hand_on(piece_of, send, recv, copies):
        if not relay:
            return
        for i, (came_by, goes_by) in enumerate(((1, 2), (2, 1))):
            half_copy(piece_of, flip(head, came_by), came_by, i, send, recv).wait_recv()
            copy = far_half(piece_of, came_by, i, send, recv, plane[goes_by])
            copy.start()
            copies.append(copy)

    def arrived(piece_of, k, send, recv):
        for i in range(2):
            if relay and k == 3:
                far_half(piece_of, 3, i, send, recv, plane[2 - i]).wait_recv()
            elif not (relay and i == k - 1):
                half_copy(piece_of, flip(head, k), k, i, send, recv).wait_recv()

    offset = shift[0]
    at_row = lax.broadcasted_iota(jnp.int32, (WIN, 2 * WIN), 0)
    at_column = lax.broadcasted_iota(jnp.int32, (WIN, 2 * WIN), 1)
    forth = (at_column == at_row + offset).astype(F32).astype(BF16)
    back = (at_column == at_row + (WIN - offset)).astype(F32).astype(BF16)

    def place_of(j):
        return (j - 1) % (blocks + 1) if j > 0 else blocks - 1

    def roll_window(j):
        to = place_of(j) if j < blocks else blocks
        rolled[to * WIN : (to + 1) * WIN, :] = dot(
            forth, extended[j * WIN : (j + 2) * WIN, :]
        ).astype(BF16)

    def project_rows(first, last):
        def project(i, carry):
            at = pl.ds(pl.multiple_of(i * 256, 256), 256)
            packed[first:last, at] = dot(rolled[first:last, :], v_qkv[:, at]).astype(BF16)
            return carry

        lax.fori_loop(0, packed.shape[1] // 256, project, 0)

    def window(place, target):
        at = pl.ds(pl.multiple_of(place * WIN, WIN), WIN)
        to = pl.ds(pl.multiple_of(target * WIN, WIN), WIN)
        for half in range(2):
            width = packed.shape[1] // 2
            parts_of = attend(packed[at, half * width : (half + 1) * width], HEADS // 2, None)
            blended[to, half * (C // 2) : (half + 1) * (C // 2)] = jnp.concatenate(parts_of, axis=1)

    inner = blocks - 1

    def windows(first, last):
        def step(i, carry):
            window(i, jnp.where(i < inner, i + 1, (i - inner) * blocks))
            return carry

        lax.fori_loop(first, last, step, 0)

    for j in range(1, blocks):
        roll_window(j)
    own[0].wait()
    project_rows(0, inner * WIN)
    windows(0, inner)
    halo_left.wait()
    halo_right.wait()
    roll_window(0)
    roll_window(blocks)
    project_rows(inner * WIN, (blocks + 1) * WIN)
    forward(PROJ, 1)
    forward(QKV, 1)
    windows(inner, blocks + 1)

    collect(PROJ, fars[:1])
    for far in fars[1:]:
        forward(PROJ, far)
    own[1].wait()
    for j in range(blocks):
        at = slice(j * WIN, (j + 1) * WIN)
        rolled[at, :] = dot(back, blended[j * WIN : (j + 2) * WIN, :]).astype(BF16)
    fine[...] = tokens[...] + dot(rolled[:rows, :], v_proj[...])
    rolled[:rows, :] = norm(fine[...]).astype(BF16)

    own[2].wait()

    def fine_hidden(i, carry):
        at = pl.ds(pl.multiple_of(i * 256, 256), 256)
        hidden[:, at] = gelu(dot(rolled[:rows, :], v_up[:, at])).astype(BF16)
        return carry

    chunks = hidden.shape[1] // 256
    lax.fori_loop(0, chunks, fine_hidden, 0)
    collect(PROJ, fars[1:2])
    for far in fars[1:]:
        forward(QKV, far)
    send_own(UP1)
    own[3].wait()

    def fine_sum(i, carry):
        at = pl.ds(pl.multiple_of(i * 256, 256), 256)
        fine[:, at] += dot(hidden[...], v_down[:, at])
        return carry

    lax.fori_loop(0, C // 256, fine_sum, 0)
    collect(PROJ, fars[2:])
    forward(UP0, 1)

    group = w_merge.shape[0] // C
    cells = rows // group
    own[4].wait()
    members = []
    for c in range(C // 128):
        lanes[c] = fine[:, c * 128 : (c + 1) * 128]
    for k in range(group):
        pieces = [lanes[c, pl.ds(k, cells, stride=group), :] for c in range(C // 128)]
        member = jnp.concatenate(pieces, axis=1)
        fine_bf[k * cells : (k + 1) * cells, :] = member.astype(BF16)
        members.append(member)
    merged = jnp.concatenate(members, axis=1)
    grouped[...] = norm(merged).astype(BF16)
    width = coarse.shape[1]

    def merge(i, carry):
        at = pl.ds(pl.multiple_of(i * 256, 256), 256)
        coarse[:, at] = dot(grouped[...], v_merge[:, at])
        return carry

    lax.fori_loop(0, width // 256, merge, 0)

    def shared_of(h):
        return shared.at[h]

    shared[head] = norm(coarse[...]).astype(BF16)
    gathers = gather(shared_of, a_send, a_recv)
    own_shards[QKV].wait()
    collect(QKV, fars)
    take_over(QKV)

    blends = []
    heads_here = g_qkv.shape[1] // (3 * HD)
    for k in range(head_count):
        target = plane[k][1]
        if k > 0:
            arrived(shared_of, k, a_send, a_recv)
        c_packed[...] = dot(shared[target], g_qkv[...]).astype(BF16)
        parts_of = attend(c_packed[...], heads_here, counts[target])
        if k == 0:
            got_blend[head] = jnp.concatenate(parts_of, axis=1)
            hand_on(shared_of, a_send, a_recv, gathers)
        else:
            sent_blend[k] = jnp.concatenate(parts_of, axis=1)
            copy = remote(sent_blend.at[k], got_blend.at[head], b_send.at[k], b_recv.at[k], plane[k])
            copy.start()
            blends.append(copy)
        if k == min(1, head_count - 1):
            forward(UP1, 1)
        if k == min(2, head_count - 1):
            for which in (UP0, UP1):
                for far in fars[1:]:
                    forward(which, far)
            send_own(DOWN)
    for s in range(chips):
        owner = ((chip + s) % chips) * 2 + core
        for k in range(1, head_count):
            piece = g_proj.at[plane[k][1], owner]
            remote(piece, piece, q_send.at[k, s], q_recv.at[k, owner // 2], plane[k]).wait_recv()
            remote(piece, piece, x_send.at[k, s], x_recv.at[k, owner // 2], partner).start()
    own_shards[PROJ].wait()
    take_over(PROJ)
    for s in range(chips):
        owner = ((chip + s) % chips) * 2 + 1 - core
        for k in range(1, head_count):
            piece = g_proj.at[plane[k][1], owner]
            remote(piece, piece, x_send.at[k, s], x_recv.at[k, owner // 2], partner).wait_recv()
    for copy in blends:
        copy.wait_recv()
    for r in range(region_count):
        w = g_proj.shape[3]
        total_of = dot(got_blend[0], g_proj[0, r])
        for h in range(1, head_count):
            total_of += dot(got_blend[h], g_proj[h, r])
        mid[:, r * w : (r + 1) * w] = coarse[:, r * w : (r + 1) * w] + total_of

    def row_block(h):
        return pl.ds(pl.multiple_of(h * cells, cells), cells)

    def normed_of(h):
        return c_normed.at[row_block(h)]

    c_normed[row_block(head), :] = norm(mid[...]).astype(BF16)
    seconds = gather(normed_of, m_send, m_recv)
    forward(DOWN, 1)
    own[5].wait()
    own[6].wait()
    for c in range(C // 256):
        at = slice(c * 256, (c + 1) * 256)
        fine[:, at] = dot(fine_bf[...], v_out[:C, at])
    hand_on(normed_of, m_send, m_recv, seconds)
    for which in (UP0, UP1):
        own_shards[which].wait()
        collect(which, fars)
        take_over(which)
    for k in range(1, head_count):
        arrived(normed_of, k, m_send, m_recv)
    for far in fars[1:]:
        forward(DOWN, far)

    def coarse_hidden(i, carry):
        at = pl.ds(pl.multiple_of(i * 256, 256), 256)
        c_hidden[:, at] = gelu(dot(c_normed[...], g_up[:, at])).astype(BF16)
        return carry

    lax.fori_loop(0, c_hidden.shape[1] // 256, coarse_hidden, 0)

    turn = 1 - 2 * (chip // ((chips + 1) // 2))
    w = g_down.shape[2]
    pair = 2 * w

    def chip_at(s):
        return (chip + turn * s + chips * chips) % chips

    own_shards[DOWN].wait()
    returns = []
    for s in range(chips):
        holder = chip_at(s)
        columns = pl.ds(pl.multiple_of(holder * pair, pair), pair)
        if s > 0:
            for far in fars:
                for way in ways:
                    @pl.when(came(way, far) & jnp.logical_not(goes(way)) & (owner_of(way, far) // 2 == holder))
                    def _():
                        arrive(DOWN, way, far, False)
        take_one(DOWN, holder * 2 + 1 - core)
        weights = jnp.concatenate([g_down[holder * 2], g_down[holder * 2 + 1]], axis=1)
        term[...] = dot(c_hidden[...], weights)
        mid[:, columns] += term[row_block(head), :]
        for k in range(1, head_count):
            parts[k, :, columns] = term[row_block(plane[k][1]), :].astype(BF16)
            copy = remote(parts.at[k, :, columns], got_parts.at[k, :, columns],
                          r_send.at[k, s], r_recv.at[k, s], plane[k])
            copy.start()
            returns.append(copy)
    for s in range(chips):
        columns = pl.ds(pl.multiple_of(chip_at(s) * pair, pair), pair)
        for k in range(1, head_count):
            returns[s * (head_count - 1) + k - 1].wait_recv()
        result = mid[:, columns]
        for k in range(1, head_count):
            result += got_parts[k, :, columns].astype(F32)
        result = result.astype(BF16)
        for k in range(group):
            at = slice(k * C, (k + 1) * C)
            piece = dot(result, v_expand[columns, at])
            if s > 0:
                piece += wide[:, at]
            if s < chips - 1:
                wide[:, at] = piece
            else:
                spread[k * cells : (k + 1) * cells, :] = piece.astype(BF16)
    for c in range(C // 128):
        at = slice(c * 128, (c + 1) * 128)
        value = fine[:, at] + dot(spread[...], v_out[C:, at])
        for k in range(group):
            lanes[c, pl.ds(k, cells, stride=group), :] = value[k * cells : (k + 1) * cells, :]
        out[:, at] = lanes[c]

    for copy in gathers + blends + seconds + returns:
        copy.wait_send()
    for which in range(5):
        for way in ways:
            @pl.when(goes(way))
            def _():
                hop(which, way, 0).wait_send()
            for far in fars[:-1]:
                @pl.when(came(way, far) & goes(way))
                def _():
                    hop(which, way, far).wait_send()
        for s in range(chips):
            pass_over(which, ((chip + s) % chips) * 2 + core).wait_send()
    for s in range(chips):
        owner = ((chip + s) % chips) * 2 + core
        for k in range(1, head_count):
            piece = g_proj.at[head, owner]
            remote(piece, piece, q_send.at[k, owner // 2], q_recv.at[k, owner // 2], plane[k]).wait_send()
            piece = g_proj.at[plane[k][1], owner]
            remote(piece, piece, x_send.at[k, s], x_recv.at[k, owner // 2], partner).wait_send()


def body(region_count, head_count, tokens, shift, counts, *weights):
    rows = tokens.shape[0]
    w_qkv, w_proj, w_up, w_down, w_merge, c_qkv, c_proj, c_up, c_down, w_expand, w_out = weights
    width = w_merge.shape[1]
    group = w_merge.shape[0] // C
    cells = rows // group
    vmem = pltpu.VMEM
    any_spec = pl.BlockSpec(memory_space=pl.ANY)
    dma = pltpu.SemaphoreType.DMA
    chips = region_count // 2
    mine = c_proj.shape[0]
    scratch = [vmem(w.shape, BF16) for w in (w_qkv, w_proj, w_up, w_down, w_merge, w_expand, w_out)]
    scratch += [
        vmem((width, c_qkv.shape[1]), BF16),
        vmem((head_count, region_count) + c_proj.shape, BF16),
        vmem((width, c_up.shape[1]), BF16),
        vmem((region_count,) + c_down.shape, BF16),
        vmem((rows + 2 * WIN, C), BF16),
        vmem((rows + WIN, C), BF16),
        vmem((rows + WIN, w_qkv.shape[1]), BF16),
        vmem((rows + WIN, C), BF16),
        vmem((rows, C), F32),
        vmem((rows, C), BF16),
        vmem((rows, w_up.shape[1]), BF16),
        vmem((cells, group * C), BF16),
        vmem((cells, width), F32),
        vmem((head_count, cells, width), BF16),
        vmem((cells, c_qkv.shape[1]), BF16),
        vmem((head_count, cells, mine), BF16),
        vmem((head_count, cells, mine), BF16),
        vmem((cells, width), F32),
        vmem((head_count * cells, width), BF16),
        vmem((head_count * cells, c_up.shape[1]), BF16),
        vmem((head_count * cells, 2 * c_down.shape[1]), F32),
        vmem((head_count, cells, width), BF16),
        vmem((head_count, cells, width), BF16),
        vmem((cells, group * C), F32),
        vmem((rows, C), BF16),
        vmem((C // 128, rows, 128), F32),
        dma((7,)), dma((2,)), dma((2,)), dma((5,)), dma((5, 2 * chips)), dma((5, region_count)), dma((5, chips)),
    ]
    scratch += [dma((head_count, chips)) for _ in range(4)]
    scratch += [
        dma((head_count, 2)), dma((head_count, 2)), dma((head_count,)), dma((head_count,)), dma((head_count, 2)),
        dma((head_count, 2)), dma((head_count, chips)), dma((head_count, chips)),
    ]
    return pl.pallas_call(
        functools.partial(kernel, region_count, head_count),
        out_shape=jax.ShapeDtypeStruct((rows, C), F32),
        in_specs=[pl.BlockSpec(memory_space=pltpu.SMEM)] * 2
        + [pl.BlockSpec(memory_space=pltpu.VMEM)] + [any_spec] * 11,
        out_specs=pl.BlockSpec(memory_space=pltpu.VMEM),
        scratch_shapes=scratch,
        compiler_params=pltpu.CompilerParams(
            collective_id=0, has_side_effects=True, vmem_limit_bytes=60 * 1024 * 1024
        ),
    )(shift, counts, tokens, *weights)


def solution(mesh):
    in_specs = (
        P(("region", "head"), None), P(), P("region"), P(), P(), P(), P(), P(),
        P("region", "head"), P("head", "region"), P("region", "head"), P("head", "region"), P(), P(),
    )
    out_specs = P(("region", "head"), None)
    run = functools.partial(body, mesh.shape["region"], mesh.shape["head"])
    return jax.shard_map(run, mesh=mesh, in_specs=in_specs, out_specs=out_specs, check_vma=False)
```

```python
import functools

import jax
import jax.numpy as jnp
from jax import lax
from jax.experimental import pallas as pl
from jax.experimental.pallas import tpu as pltpu
from jax.sharding import PartitionSpec as P

C = 512
HD = 64
HF = 8
WIN = 144
HEADS = HF
MESH = pl.DeviceIdType.MESH
F32 = jnp.float32
BF16 = jnp.bfloat16
LOG2E = 1.4426950408889634


def norm(values):
    average = jnp.mean(values, axis=-1, keepdims=True)
    centred = values - average
    spread = jnp.mean(centred * centred, axis=-1, keepdims=True)
    return centred * lax.rsqrt(spread + 1e-05)


def gelu(values):
    return 0.5 * values * (1.0 + lax.erf(values * (0.5**0.5)))


def dot(left, right):
    return jnp.dot(left, right, preferred_element_type=F32)


def flip(index, mask):
    result = index
    bit = 1
    while bit <= mask:
        if mask & bit:
            result = result + (1 - 2 * ((index // bit) % 2)) * bit
        bit *= 2
    return result


def attend(packed, head_count, visible):
    scale = HD**-0.5
    blended = []
    for head in range(head_count):
        base = head * 3 * HD
        query = packed[:, base : base + HD]
        key = packed[:, base + HD : base + 2 * HD]
        value = packed[:, base + 2 * HD : base + 3 * HD]
        scores = lax.dot_general(
            key, query, (((1,), (1,)), ((), ())), preferred_element_type=F32
        )
        if visible is not None:
            scores = jnp.where(visible, scores, -1e30 / scale)
        raised = jnp.exp2((scores - jnp.max(scores, axis=0, keepdims=True)) * (scale * LOG2E))
        weights = (raised * (1.0 / jnp.sum(raised, axis=0, keepdims=True))).astype(BF16)
        mixed = lax.dot_general(
            weights, value, (((0,), (0,)), ((), ())), preferred_element_type=F32
        )
        blended.append(mixed.astype(BF16))
    return blended


def kernel(
    region_count, head_count,
    shift, counts, tokens, w_qkv, w_proj, w_up, w_down, w_merge,
    c_qkv, c_proj, c_up, c_down, w_expand, w_out,
    out,
    v_qkv, v_proj, v_up, v_down, v_merge, v_expand, v_out,
    g_qkv, g_proj, g_up, g_down,
    extended, rolled, packed, blended, fine, fine_bf, hidden,
    coarse, shared, sent_blend, got_blend, mid, c_normed, c_hidden, parts, got_parts,
    wide, spread, lanes,
    local_sem, halo_send, halo_recv, own_sem, z_send, w_recv, p_send, q_send, q_recv, x_send, x_recv,
    a_send, a_recv, b_send, b_recv, m_send, m_recv, r_send, r_recv,
):
    region, head = lax.axis_index("region"), lax.axis_index("head")
    chips = region_count // 2
    chip, core = region // 2, region % 2
    rows = tokens.shape[0]
    blocks = rows // WIN
    flat = region * head_count + head
    total = region_count * head_count
    before, after = (flat + total - 1) % total, (flat + 1) % total
    before = (before // head_count, before % head_count)
    after = (after // head_count, after % head_count)
    partner = (chip * 2 + 1 - core, head)
    plane = [(region, flip(head, k)) for k in range(head_count)]
    ways = (1, -1)

    def line(way):
        return (((chip + way + chips) % chips) * 2 + core, head)

    barrier = pltpu.get_barrier_semaphore()
    greeted = [before, after, partner, line(1), line(-1)] + plane[1:]
    for device in greeted:
        pl.semaphore_signal(barrier, inc=1, device_id=device, device_id_type=MESH)

    QKV, PROJ, UP0, UP1, DOWN = range(5)
    half_up = c_up.shape[0] // 2
    shards = [c_qkv, c_proj, c_up.at[pl.ds(0, half_up)], c_up.at[pl.ds(half_up, half_up)], c_down]

    def slot(which, owner):
        if which == QKV:
            return g_qkv.at[pl.ds(owner * c_qkv.shape[0], c_qkv.shape[0])]
        if which == PROJ:
            return g_proj.at[head, owner]
        if which == UP0:
            return g_up.at[pl.ds(owner * c_up.shape[0], half_up)]
        if which == UP1:
            return g_up.at[pl.ds(owner * c_up.shape[0] + half_up, half_up)]
        return g_down.at[owner]

    own_shards = []
    for which in range(5):
        own_shards.append(pltpu.make_async_copy(shards[which], slot(which, region), own_sem.at[which]))
    own = []
    for at, (source, target) in enumerate(
        [(w_qkv, v_qkv), (w_proj, v_proj), (w_up, v_up), (w_down, v_down), (w_merge, v_merge),
         (w_expand, v_expand), (w_out, v_out)]
    ):
        own.append(pltpu.make_async_copy(source, target, local_sem.at[at]))
    for copy in (own_shards[0], own_shards[1], own[0], own[1]):
        copy.start()

    def remote(source, target, send, recv, device):
        return pltpu.make_async_remote_copy(
            src_ref=source, dst_ref=target, send_sem=send, recv_sem=recv,
            device_id=device, device_id_type=MESH,
        )

    extended[WIN : WIN + rows, :] = norm(tokens[...]).astype(BF16)
    pl.semaphore_wait(barrier, len(greeted))

    halo_left = remote(extended.at[pl.ds(WIN, WIN)], extended.at[pl.ds(WIN + rows, WIN)],
                       halo_send.at[0], halo_recv.at[0], before)
    halo_right = remote(extended.at[pl.ds(rows, WIN)], extended.at[pl.ds(0, WIN)],
                        halo_send.at[1], halo_recv.at[1], after)
    halo_left.start()
    halo_right.start()

    def came(way, far):
        return (chip - way * far >= 0) & (chip - way * far < chips)

    def goes(way):
        return (chip + way >= 0) & (chip + way < chips)

    def owner_of(way, far):
        return ((chip - way * far + chips * chips) % chips) * 2 + core

    def hop(which, way, far):
        owner = owner_of(way, far)
        place = slot(which, owner)
        return remote(place, place,
                      z_send.at[which, (way < 0) * chips + far], w_recv.at[which, owner], line(way))

    def pass_over(which, owner):
        place = slot(which, owner)
        return remote(place, place, p_send.at[which, owner // 2], w_recv.at[which, owner], partner)

    def chip_at(s):
        if chips != 4:
            return (chip + s) % chips
        side = chip // 2
        return (chip, flip(chip, 1), 2 * (1 - side) + side, 2 * (1 - side) + 1 - side)[s]

    def spread_proj(s):
        owner = chip_at(s) * 2 + core
        for k in range(1, head_count):
            piece = g_proj.at[head, owner]
            remote(piece, piece, q_send.at[k, owner // 2], q_recv.at[k, owner // 2], plane[k]).start()

    def send_own(which):
        for way in ways:
            @pl.when(goes(way))
            def _():
                hop(which, way, 0).start()

    def arrive(which, way, far, forward):
        owner = owner_of(way, far)
        remote(slot(which, owner), slot(which, owner), p_send.at[which, owner // 2],
               w_recv.at[which, owner], line(way)).wait_recv()
        if forward:
            hop(which, way, far).start()
        pass_over(which, owner).start()

    def forward(which, far):
        if far > chips - 2:
            return
        for way in ways:
            @pl.when(came(way, far) & goes(way))
            def _():
                arrive(which, way, far, True)

    def collect(which, fars):
        for far in fars:
            for way in ways:
                @pl.when(came(way, far) & jnp.logical_not(goes(way)))
                def _():
                    arrive(which, way, far, False)

    def take_one(which, owner):
        remote(slot(which, owner), slot(which, owner), p_send.at[which, owner // 2],
               w_recv.at[which, owner], partner).wait_recv()

    def take_over(which):
        for s in range(chips):
            take_one(which, ((chip + s) % chips) * 2 + 1 - core)

    fars = range(1, chips)

    for which in (QKV, PROJ):
        own_shards[which].wait()
        send_own(which)
        pass_over(which, region).start()
    for copy in own[2:5] + own_shards[2:] + own[5:]:
        copy.start()

    relay = head_count == 4

    def half_of(piece_of, h, i):
        whole = piece_of(h)
        half = whole.shape[1] // 2
        return whole.at[:, pl.ds(i * half, half)]

    def half_copy(piece_of, h, k, i, send, recv):
        piece = half_of(piece_of, h, i)
        return remote(piece, piece, send.at[k, i], recv.at[k, i], plane[k])

    def gather(piece_of, send, recv):
        copies = []
        for i in range(2):
            for k in range(1, 3 if relay else head_count):
                copy = half_copy(piece_of, head, k, i if k != 2 else 1 - i, send, recv)
                copy.start()
                copies.append(copy)
        return copies

    def far_half(piece_of, mask, i, send, recv, device):
        piece = half_of(piece_of, flip(head, mask), i)
        return remote(piece, piece, send.at[3, i], recv.at[3, i], device)

    def hand_on(piece_of, send, recv, copies):
        if not relay:
            return
        for i, (came_by, goes_by) in enumerate(((1, 2), (2, 1))):
            half_copy(piece_of, flip(head, came_by), came_by, i, send, recv).wait_recv()
            copy = far_half(piece_of, came_by, i, send, recv, plane[goes_by])
            copy.start()
            copies.append(copy)

    def arrived(piece_of, k, send, recv):
        for i in range(2):
            if relay and k == 3:
                far_half(piece_of, 3, i, send, recv, plane[2 - i]).wait_recv()
            elif not (relay and i == k - 1):
                half_copy(piece_of, flip(head, k), k, i, send, recv).wait_recv()

    offset = shift[0]
    at_row = lax.broadcasted_iota(jnp.int32, (WIN, 2 * WIN), 0)
    at_column = lax.broadcasted_iota(jnp.int32, (WIN, 2 * WIN), 1)
    forth = (at_column == at_row + offset).astype(F32).astype(BF16)
    back = (at_column == at_row + (WIN - offset)).astype(F32).astype(BF16)

    def place_of(j):
        return (j - 1) % (blocks + 1) if j > 0 else blocks - 1

    def roll_window(j):
        to = place_of(j) if j < blocks else blocks
        rolled[to * WIN : (to + 1) * WIN, :] = dot(
            forth, extended[j * WIN : (j + 2) * WIN, :]
        ).astype(BF16)

    def project_rows(first, last):
        packed[first:last, :] = dot(rolled[first:last, :], v_qkv[...]).astype(BF16)

    inner = blocks - 1

    def windows(first, last):
        for place in range(first, last):
            target = place + 1 if place < inner else (place - inner) * blocks
            at = slice(place * WIN, (place + 1) * WIN)
            blended[target * WIN : (target + 1) * WIN, :] = jnp.concatenate(
                attend(packed[at, :], HEADS, None), axis=1
            )

    group = w_merge.shape[0] // C
    cells = rows // group
    width = coarse.shape[1]
    near, edge = list(range(1, blocks - 1)), [0, blocks - 1]
    order = near + edge
    spans = [(0, len(near) * WIN), (len(near) * WIN, rows)]

    def fine_chunk(index):
        first, last = spans[index]
        members_of = (near, edge)[index]
        for p, j in enumerate(members_of):
            rolled[first + p * WIN : first + (p + 1) * WIN, :] = dot(
                back, blended[j * WIN : (j + 2) * WIN, :]
            ).astype(BF16)
        own[1].wait() if index == 0 else None
        attended = dot(rolled[first:last, :], v_proj[...])
        for p, j in enumerate(members_of):
            fine[first + p * WIN : first + (p + 1) * WIN, :] = (
                tokens[j * WIN : (j + 1) * WIN, :] + attended[p * WIN : (p + 1) * WIN, :]
            )
        rolled[first:last, :] = norm(fine[first:last, :]).astype(BF16)
        own[2].wait() if index == 0 else None
        hidden[first:last, :] = gelu(dot(rolled[first:last, :], v_up[...])).astype(BF16)
        own[3].wait() if index == 0 else None
        fine[first:last, :] += dot(hidden[first:last, :], v_down[...])

    def merge_chunk(index):
        first, last = spans[index]
        low, high = first // group, last // group
        for c in range(C // 128):
            lanes[c, first:last, :] = fine[first:last, c * 128 : (c + 1) * 128]
        members = []
        for k in range(group):
            pieces = [lanes[c, pl.ds(first + k, high - low, stride=group), :] for c in range(C // 128)]
            members.append(jnp.concatenate(pieces, axis=1))
        fine_bf[first:last, :] = jnp.concatenate(members, axis=0).astype(BF16)
        own[4].wait() if index == 0 else None
        coarse[low:high, :] = dot(norm(jnp.concatenate(members, axis=1)).astype(BF16), v_merge[...])
        shared[index, head] = norm(coarse[low:high, :]).astype(BF16)

    def shared_of(index):
        return lambda h: shared.at[index, h]

    for j in range(1, blocks):
        roll_window(j)
    own[0].wait()
    project_rows(0, inner * WIN)
    windows(0, inner)
    fine_chunk(0)
    forward(QKV, 1)
    merge_chunk(0)
    gathers = gather(shared_of(0), a_send.at[0], a_recv.at[0])
    halo_left.wait()
    halo_right.wait()
    forward(PROJ, 1)
    collect(PROJ, fars[:1])
    for s in range(min(2, chips)):
        spread_proj(s)
    roll_window(0)
    roll_window(blocks)
    project_rows(inner * WIN, (blocks + 1) * WIN)
    windows(inner, blocks + 1)
    for far in fars[1:]:
        forward(QKV, far)
    for which in (UP0, UP1, DOWN):
        own_shards[which].wait()
        pass_over(which, region).start()
    send_own(UP0)
    hand_on(shared_of(0), a_send.at[0], a_recv.at[0], gathers)
    fine_chunk(1)
    for far in fars[1:]:
        forward(PROJ, far)
    merge_chunk(1)
    gathers += gather(shared_of(1), a_send.at[1], a_recv.at[1])
    send_own(UP1)
    collect(QKV, fars)
    take_over(QKV)

    at_key = lax.broadcasted_iota(jnp.int32, (cells, cells), 0)
    block_cells = WIN // group
    inside = len(near) * block_cells
    place = jnp.where(
        at_key < inside, at_key + block_cells, jnp.where(at_key < inside + block_cells, at_key - inside, at_key)
    )

    blends = []
    heads_here = g_qkv.shape[1] // (3 * HD)

    def coarse_attention(ks):
        packed_of = [
            jnp.concatenate(
                [dot(shared[index, plane[k][1]], g_qkv[...]) for index in range(2)], axis=0
            ).astype(BF16)
            for k in ks
        ]
        for k, its in zip(ks, packed_of):
            parts_of = attend(its, heads_here, place < counts[plane[k][1]])
            if k == 0:
                got_blend[head] = jnp.concatenate(parts_of, axis=1)
            else:
                sent_blend[k] = jnp.concatenate(parts_of, axis=1)

    forward(UP0, 1)
    coarse_attention([0])
    hand_on(shared_of(1), a_send.at[1], a_recv.at[1], gathers)
    collect(PROJ, fars[1:])
    for s in range(2, chips):
        spread_proj(s)
    forward(UP1, 1)
    for far in fars[1:]:
        forward(UP0, far)
    send_own(DOWN)
    for ks in [range(1, min(3, head_count)), range(3, head_count)]:
        for k in ks:
            for index in range(2):
                arrived(shared_of(index), k, a_send.at[index], a_recv.at[index])
        coarse_attention(ks)
        for k in ks:
            copy = remote(sent_blend.at[k], got_blend.at[head], b_send.at[k], b_recv.at[k], plane[k])
            copy.start()
            blends.append(copy)
        if 1 in ks:
            for far in fars[1:]:
                forward(UP1, far)
    forward(DOWN, 1)
    for s in range(chips):
        owner = ((chip + s) % chips) * 2 + core
        for k in range(1, head_count):
            piece = g_proj.at[plane[k][1], owner]
            remote(piece, piece, q_send.at[k, s], q_recv.at[k, owner // 2], plane[k]).wait_recv()
            remote(piece, piece, x_send.at[k, s], x_recv.at[k, owner // 2], partner).start()
    take_over(PROJ)
    for s in range(chips):
        owner = ((chip + s) % chips) * 2 + 1 - core
        for k in range(1, head_count):
            piece = g_proj.at[plane[k][1], owner]
            remote(piece, piece, x_send.at[k, s], x_recv.at[k, owner // 2], partner).wait_recv()
    for copy in blends:
        copy.wait_recv()
    for r in range(region_count):
        w = g_proj.shape[3]
        total_of = dot(got_blend[0], g_proj[0, r])
        for h in range(1, head_count):
            total_of += dot(got_blend[h], g_proj[h, r])
        mid[:, r * w : (r + 1) * w] = coarse[:, r * w : (r + 1) * w] + total_of

    def row_block(h):
        return pl.ds(pl.multiple_of(h * cells, cells), cells)

    def normed_of(h):
        return c_normed.at[row_block(h)]

    c_normed[row_block(head), :] = norm(mid[...]).astype(BF16)
    seconds = gather(normed_of, m_send, m_recv)
    for far in fars[1:]:
        forward(DOWN, far)
    own[5].wait()
    own[6].wait()
    for c in range(C // 256):
        at = slice(c * 256, (c + 1) * 256)
        fine[:, at] = dot(fine_bf[...], v_out[:C, at])
    hand_on(normed_of, m_send, m_recv, seconds)
    for which in (UP0, UP1):
        collect(which, fars)
        take_over(which)
    w = g_down.shape[2]
    pair = 2 * w
    returns = []

    def columns_of(s):
        return pl.ds(pl.multiple_of(chip_at(s) * pair, pair), pair)

    def down_ready(s):
        holder = chip_at(s)
        if s > 0:
            for far in fars:
                for way in ways:
                    @pl.when(came(way, far) & jnp.logical_not(goes(way)) & (owner_of(way, far) // 2 == holder))
                    def _():
                        arrive(DOWN, way, far, False)
        take_one(DOWN, holder * 2 + 1 - core)

    def down(k, s):
        holder = chip_at(s)
        weights = jnp.concatenate([g_down[holder * 2], g_down[holder * 2 + 1]], axis=1)
        product = dot(c_hidden[row_block(plane[k][1]), :], weights)
        if k == 0:
            mid[:, columns_of(s)] += product
        else:
            parts[k, :, columns_of(s)] = product.astype(BF16)

    def send_back(k, s):
        copy = remote(parts.at[k, :, columns_of(s)], got_parts.at[k, :, columns_of(s)],
                      r_send.at[k, s], r_recv.at[k, s], plane[k])
        copy.start()
        returns.append(copy)

    early = min(2, chips)
    for k in range(head_count):
        at = row_block(plane[k][1])
        if k > 0:
            arrived(normed_of, k, m_send, m_recv)
        c_hidden[at, :] = gelu(dot(c_normed[at, :], g_up[...])).astype(BF16)
        for s in range(early):
            if k == 0:
                down_ready(s)
        for s in range(early):
            down(k, s)
            if k > 0:
                send_back(k, s)
    for s in range(early, chips):
        down_ready(s)
        for k in [*range(1, head_count), 0]:
            down(k, s)
            if k > 0:
                send_back(k, s)
    for s in range(chips):
        columns = columns_of(s)
        for k in range(1, head_count):
            remote(parts.at[k, :, columns], got_parts.at[k, :, columns],
                   r_send.at[k, s], r_recv.at[k, s], plane[k]).wait_recv()
        result = mid[:, columns]
        for k in range(1, head_count):
            result += got_parts[k, :, columns].astype(F32)
        result = result.astype(BF16)
        for k in range(group):
            at = slice(k * C, (k + 1) * C)
            piece = dot(result, v_expand[columns, at])
            if s > 0:
                piece += wide[:, at]
            wide[:, at] = piece
    for first, last in spans:
        low, high = first // group, last // group
        spread[first:last, :] = jnp.concatenate(
            [wide[low:high, k * C : (k + 1) * C] for k in range(group)], axis=0
        ).astype(BF16)
    for c in range(C // 128):
        at = slice(c * 128, (c + 1) * 128)
        value = fine[:, at] + dot(spread[...], v_out[C:, at])
        for first, last in spans:
            count = (last - first) // group
            for k in range(group):
                lanes[c, pl.ds(first + k, count, stride=group), :] = value[first + k * count : first + (k + 1) * count, :]
        for p, j in enumerate(order):
            out[j * WIN : (j + 1) * WIN, at] = lanes[c, p * WIN : (p + 1) * WIN, :]

    for copy in gathers + blends + seconds + returns:
        copy.wait_send()
    for which in range(5):
        for way in ways:
            @pl.when(goes(way))
            def _():
                hop(which, way, 0).wait_send()
            for far in fars[:-1]:
                @pl.when(came(way, far) & goes(way))
                def _():
                    hop(which, way, far).wait_send()
        for s in range(chips):
            pass_over(which, ((chip + s) % chips) * 2 + core).wait_send()
    for s in range(chips):
        owner = ((chip + s) % chips) * 2 + core
        for k in range(1, head_count):
            piece = g_proj.at[head, owner]
            remote(piece, piece, q_send.at[k, owner // 2], q_recv.at[k, owner // 2], plane[k]).wait_send()
            piece = g_proj.at[plane[k][1], owner]
            remote(piece, piece, x_send.at[k, s], x_recv.at[k, owner // 2], partner).wait_send()


def body(region_count, head_count, tokens, shift, counts, *weights):
    rows = tokens.shape[0]
    w_qkv, w_proj, w_up, w_down, w_merge, c_qkv, c_proj, c_up, c_down, w_expand, w_out = weights
    width = w_merge.shape[1]
    group = w_merge.shape[0] // C
    cells = rows // group
    vmem = pltpu.VMEM
    any_spec = pl.BlockSpec(memory_space=pl.ANY)
    dma = pltpu.SemaphoreType.DMA
    chips = region_count // 2
    mine = c_proj.shape[0]
    scratch = [vmem(w.shape, BF16) for w in (w_qkv, w_proj, w_up, w_down, w_merge, w_expand, w_out)]
    scratch += [
        vmem((width, c_qkv.shape[1]), BF16),
        vmem((head_count, region_count) + c_proj.shape, BF16),
        vmem((width, c_up.shape[1]), BF16),
        vmem((region_count,) + c_down.shape, BF16),
        vmem((rows + 2 * WIN, C), BF16),
        vmem((rows + WIN, C), BF16),
        vmem((rows + WIN, w_qkv.shape[1]), BF16),
        vmem((rows + WIN, C), BF16),
        vmem((rows, C), F32),
        vmem((rows, C), BF16),
        vmem((rows, w_up.shape[1]), BF16),
        vmem((cells, width), F32),
        vmem((2, head_count, cells // 2, width), BF16),
        vmem((head_count, cells, mine), BF16),
        vmem((head_count, cells, mine), BF16),
        vmem((cells, width), F32),
        vmem((head_count * cells, width), BF16),
        vmem((head_count * cells, c_up.shape[1]), BF16),
        vmem((head_count, cells, width), BF16),
        vmem((head_count, cells, width), BF16),
        vmem((cells, group * C), F32),
        vmem((rows, C), BF16),
        vmem((C // 128, rows, 128), F32),
        dma((7,)), dma((2,)), dma((2,)), dma((5,)), dma((5, 2 * chips)), dma((5, region_count)), dma((5, chips)),
    ]
    scratch += [dma((head_count, chips)) for _ in range(4)]
    scratch += [
        dma((2, head_count, 2)), dma((2, head_count, 2)), dma((head_count,)), dma((head_count,)), dma((head_count, 2)),
        dma((head_count, 2)), dma((head_count, chips)), dma((head_count, chips)),
    ]
    return pl.pallas_call(
        functools.partial(kernel, region_count, head_count),
        out_shape=jax.ShapeDtypeStruct((rows, C), F32),
        in_specs=[pl.BlockSpec(memory_space=pltpu.SMEM)] * 2
        + [pl.BlockSpec(memory_space=pltpu.VMEM)] + [any_spec] * 11,
        out_specs=pl.BlockSpec(memory_space=pltpu.VMEM),
        scratch_shapes=scratch,
        compiler_params=pltpu.CompilerParams(
            collective_id=0, has_side_effects=True, vmem_limit_bytes=60 * 1024 * 1024
        ),
    )(shift, counts, tokens, *weights)


def solution(mesh):
    in_specs = (
        P(("region", "head"), None), P(), P("region"), P(), P(), P(), P(), P(),
        P("region", "head"), P("head", "region"), P("region", "head"), P("head", "region"), P(), P(),
    )
    out_specs = P(("region", "head"), None)
    run = functools.partial(body, mesh.shape["region"], mesh.shape["head"])
    return jax.shard_map(run, mesh=mesh, in_specs=in_specs, out_specs=out_specs, check_vma=False)
```

```python
import functools

import jax
import jax.numpy as jnp
from jax import lax
from jax.experimental import pallas as pl
from jax.experimental.pallas import tpu as pltpu
from jax.sharding import PartitionSpec as P

C = 512
HD = 64
HF = 8
WIN = 144
HEADS = HF
MESH = pl.DeviceIdType.MESH
F32 = jnp.float32
BF16 = jnp.bfloat16
LOG2E = 1.4426950408889634


def norm(values):
    average = jnp.mean(values, axis=-1, keepdims=True)
    centred = values - average
    spread = jnp.mean(centred * centred, axis=-1, keepdims=True)
    return centred * lax.rsqrt(spread + 1e-05)


def gelu(values):
    return 0.5 * values * (1.0 + lax.erf(values * (0.5**0.5)))


def dot(left, right):
    return jnp.dot(left, right, preferred_element_type=F32)


def flip(index, mask):
    result = index
    bit = 1
    while bit <= mask:
        if mask & bit:
            result = result + (1 - 2 * ((index // bit) % 2)) * bit
        bit *= 2
    return result


def attend(packed, head_count, visible):
    scale = HD**-0.5
    blended = []
    for head in range(head_count):
        base = head * 3 * HD
        query = packed[:, base : base + HD]
        key = packed[:, base + HD : base + 2 * HD]
        value = packed[:, base + 2 * HD : base + 3 * HD]
        scores = lax.dot_general(
            key, query, (((1,), (1,)), ((), ())), preferred_element_type=F32
        )
        if visible is not None:
            scores = jnp.where(visible, scores, -1e30 / scale)
        raised = jnp.exp2((scores - jnp.max(scores, axis=0, keepdims=True)) * (scale * LOG2E))
        weights = (raised * (1.0 / jnp.sum(raised, axis=0, keepdims=True))).astype(BF16)
        mixed = lax.dot_general(
            weights, value, (((0,), (0,)), ((), ())), preferred_element_type=F32
        )
        blended.append(mixed.astype(BF16))
    return blended


def kernel(
    region_count, head_count,
    shift, counts, tokens_in, w_qkv, w_proj, w_up, w_down, w_merge,
    c_qkv, c_proj, c_up, c_down, w_expand, w_out,
    out,
    tokens, v_qkv, v_proj, v_up, v_down, v_merge, v_expand, v_out,
    g_qkv, g_proj, g_up, g_down,
    extended, rolled, packed, blended, fine, fine_bf, hidden,
    coarse, shared, sent_blend, got_blend, mid, c_normed, c_hidden, parts, got_parts,
    wide, spread, lanes,
    local_sem, halo_send, halo_recv, own_sem, z_send, z_recv, p_send, p_recv, q_send, q_recv, x_send, x_recv,
    a_send, a_recv, b_send, b_recv, m_send, m_recv, r_send, r_recv,
):
    region, head = lax.axis_index("region"), lax.axis_index("head")
    chips = region_count // 2
    chip, core = region // 2, region % 2
    rows = tokens.shape[0]
    blocks = rows // WIN
    flat = region * head_count + head
    total = region_count * head_count
    before, after = (flat + total - 1) % total, (flat + 1) % total
    before = (before // head_count, before % head_count)
    after = (after // head_count, after % head_count)
    partner = (chip * 2 + 1 - core, head)
    plane = [(region, flip(head, k)) for k in range(head_count)]
    ways = (1, -1)

    def line(way):
        return (((chip + way + chips) % chips) * 2 + core, head)

    barrier = pltpu.get_barrier_semaphore()
    greeted = [before, after, partner, line(1), line(-1)] + plane[1:]
    for device in greeted:
        pl.semaphore_signal(barrier, inc=1, device_id=device, device_id_type=MESH)

    QKV, PROJ, UP0, UP1, DOWN = range(5)
    half_up = c_up.shape[0] // 2
    shards = [c_qkv, c_proj, c_up.at[pl.ds(0, half_up)], c_up.at[pl.ds(half_up, half_up)], c_down]

    def slot(which, owner):
        if which == QKV:
            return g_qkv.at[pl.ds(owner * c_qkv.shape[0], c_qkv.shape[0])]
        if which == PROJ:
            return g_proj.at[head, owner]
        if which == UP0:
            return g_up.at[pl.ds(owner * c_up.shape[0], half_up)]
        if which == UP1:
            return g_up.at[pl.ds(owner * c_up.shape[0] + half_up, half_up)]
        return g_down.at[owner]

    token_load = pltpu.make_async_copy(tokens_in, tokens, local_sem.at[7])
    token_load.start()

    own_shards = []
    for which in range(5):
        own_shards.append(pltpu.make_async_copy(shards[which], slot(which, region), own_sem.at[which]))
    own = []
    for at, (source, target) in enumerate(
        [(w_qkv, v_qkv), (w_proj, v_proj), (w_up, v_up), (w_down, v_down), (w_merge, v_merge),
         (w_expand, v_expand), (w_out, v_out)]
    ):
        own.append(pltpu.make_async_copy(source, target, local_sem.at[at]))
    for copy in (own_shards[0], own_shards[1], own[0], own[1]):
        copy.start()

    def remote(source, target, send, recv, device):
        return pltpu.make_async_remote_copy(
            src_ref=source, dst_ref=target, send_sem=send, recv_sem=recv,
            device_id=device, device_id_type=MESH,
        )

    def received(place, sem):
        remote(place, place, sem, sem, partner).wait_recv()

    def sent(place, sem):
        remote(place, place, sem, sem, partner).wait_send()

    def stack(which, n):
        if which == QKV:
            return g_qkv.at[pl.ds(0, n * c_qkv.shape[0])]
        if which == PROJ:
            return g_proj.at[0, pl.ds(0, n)]
        if which == DOWN:
            return g_down.at[pl.ds(0, n)]
        return g_up.at[pl.ds(0, n * half_up)]

    token_load.wait()
    extended[WIN : WIN + rows, :] = norm(tokens[...]).astype(BF16)
    pl.semaphore_wait(barrier, len(greeted))

    halo_left = remote(extended.at[pl.ds(WIN, WIN)], extended.at[pl.ds(WIN + rows, WIN)],
                       halo_send, halo_recv, before)
    halo_right = remote(extended.at[pl.ds(rows, WIN)], extended.at[pl.ds(0, WIN)],
                        halo_send, halo_recv, after)
    halo_left.start()
    halo_right.start()

    def came(way, far):
        return (chip - way * far >= 0) & (chip - way * far < chips)

    def goes(way):
        return (chip + way >= 0) & (chip + way < chips)

    def owner_of(way, far):
        return ((chip - way * far + chips * chips) % chips) * 2 + core

    def hop(which, way, far):
        owner = owner_of(way, far)
        place = slot(which, owner)
        return remote(place, place, z_send.at[which], z_recv.at[which, owner // 2], line(way))

    def pass_over(which, owner):
        place = slot(which, owner)
        arrival = p_recv.at[which + owner // 2 if which == DOWN else which]
        return remote(place, place, p_send.at[which], arrival, partner)

    def chip_at(s):
        if chips != 4:
            return (chip + s) % chips
        side = chip // 2
        return (chip, flip(chip, 1), 2 * (1 - side) + side, 2 * (1 - side) + 1 - side)[s]

    def spread_proj(s):
        owner = chip_at(s) * 2 + core
        for k in range(1, head_count):
            piece = g_proj.at[head, owner]
            remote(piece, piece, q_send, q_recv, plane[k]).start()

    def send_own(which):
        for way in ways:
            @pl.when(goes(way))
            def _():
                hop(which, way, 0).start()

    def arrive(which, way, far, forward):
        owner = owner_of(way, far)
        received(slot(which, owner), z_recv.at[which, owner // 2])
        if forward:
            hop(which, way, far).start()
        pass_over(which, owner).start()

    def forward(which, far):
        if far > chips - 2:
            return
        for way in ways:
            @pl.when(came(way, far) & goes(way))
            def _():
                arrive(which, way, far, True)

    def collect(which, fars):
        for far in fars:
            for way in ways:
                @pl.when(came(way, far) & jnp.logical_not(goes(way)))
                def _():
                    arrive(which, way, far, False)

    def take_over(which):
        received(stack(which, chips), p_recv.at[which])

    fars = range(1, chips)

    for which in (QKV, PROJ):
        own_shards[which].wait()
        send_own(which)
        pass_over(which, region).start()
    for copy in own[2:5] + own_shards[2:] + own[5:]:
        copy.start()

    relay = head_count == 4

    def half_of(piece_of, h, i):
        whole = piece_of(h)
        half = whole.shape[1] // 2
        return whole.at[:, pl.ds(i * half, half)]

    def gather(piece_of, send, recv):
        for i in range(2):
            for k in range(1, 3 if relay else head_count):
                which = i if k != 2 else 1 - i
                piece = half_of(piece_of, head, which)
                lane = recv.at[(k - 1 if which == k - 1 else 2) if relay else k]
                remote(piece, piece, send, lane, plane[k]).start()

    def hand_on(piece_of, send, recv):
        if not relay:
            return
        for i, (came_by, goes_by) in enumerate(((1, 2), (2, 1))):
            piece = half_of(piece_of, flip(head, came_by), i)
            received(piece, recv.at[i])
            remote(piece, piece, send, recv.at[3], plane[goes_by]).start()

    def arrived(piece_of, k, recv):
        if not relay or k == 3:
            received(piece_of(flip(head, k)), recv.at[k])
        elif k == 1:
            received(piece_of(head), recv.at[2])

    offset = shift[0]
    at_row = lax.broadcasted_iota(jnp.int32, (WIN, 2 * WIN), 0)
    at_column = lax.broadcasted_iota(jnp.int32, (WIN, 2 * WIN), 1)
    forth = (at_column == at_row + offset).astype(F32).astype(BF16)
    back = (at_column == at_row + (WIN - offset)).astype(F32).astype(BF16)

    def place_of(j):
        return (j - 1) % (blocks + 1) if j > 0 else blocks - 1

    def roll_window(j):
        to = place_of(j) if j < blocks else blocks
        rolled[to * WIN : (to + 1) * WIN, :] = dot(
            forth, extended[j * WIN : (j + 2) * WIN, :]
        ).astype(BF16)

    def project_rows(first, last):
        packed[first:last, :] = dot(rolled[first:last, :], v_qkv[...]).astype(BF16)

    inner = blocks - 1

    def windows(first, last):
        for place in range(first, last):
            target = place + 1 if place < inner else (place - inner) * blocks
            at = slice(place * WIN, (place + 1) * WIN)
            blended[target * WIN : (target + 1) * WIN, :] = jnp.concatenate(
                attend(packed[at, :], HEADS, None), axis=1
            )

    group = w_merge.shape[0] // C
    cells = rows // group
    width = coarse.shape[1]
    near, edge = list(range(1, blocks - 1)), [0, blocks - 1]
    order = near + edge
    spans = [(0, len(near) * WIN), (len(near) * WIN, rows)]

    def fine_chunk(index):
        first, last = spans[index]
        members_of = (near, edge)[index]
        for p, j in enumerate(members_of):
            rolled[first + p * WIN : first + (p + 1) * WIN, :] = dot(
                back, blended[j * WIN : (j + 2) * WIN, :]
            ).astype(BF16)
        own[1].wait() if index == 0 else None
        attended = dot(rolled[first:last, :], v_proj[...])
        for p, j in enumerate(members_of):
            fine[first + p * WIN : first + (p + 1) * WIN, :] = (
                tokens[j * WIN : (j + 1) * WIN, :] + attended[p * WIN : (p + 1) * WIN, :]
            )
        rolled[first:last, :] = norm(fine[first:last, :]).astype(BF16)
        own[2].wait() if index == 0 else None
        hidden[first:last, :] = gelu(dot(rolled[first:last, :], v_up[...])).astype(BF16)
        own[3].wait() if index == 0 else None
        fine[first:last, :] += dot(hidden[first:last, :], v_down[...])

    def merge_chunk(index):
        first, last = spans[index]
        low, high = first // group, last // group
        for c in range(C // 128):
            lanes[c, first:last, :] = fine[first:last, c * 128 : (c + 1) * 128]
        members = []
        for k in range(group):
            pieces = [lanes[c, pl.ds(first + k, high - low, stride=group), :] for c in range(C // 128)]
            members.append(jnp.concatenate(pieces, axis=1))
        fine_bf[first:last, :] = jnp.concatenate(members, axis=0).astype(BF16)
        own[4].wait() if index == 0 else None
        coarse[low:high, :] = dot(norm(jnp.concatenate(members, axis=1)).astype(BF16), v_merge[...])
        shared[index, head] = norm(coarse[low:high, :]).astype(BF16)

    def shared_of(index):
        return lambda h: shared.at[index, h]

    for j in range(1, blocks):
        roll_window(j)
    own[0].wait()
    project_rows(0, inner * WIN)
    windows(0, inner)
    fine_chunk(0)
    forward(QKV, 1)
    merge_chunk(0)
    gather(shared_of(0), a_send, a_recv.at[0])
    received(extended.at[pl.ds(0, 2 * WIN)], halo_recv)
    forward(PROJ, 1)
    collect(PROJ, fars[:1])
    for s in range(min(2, chips)):
        spread_proj(s)
    roll_window(0)
    roll_window(blocks)
    project_rows(inner * WIN, (blocks + 1) * WIN)
    windows(inner, blocks + 1)
    for far in fars[1:]:
        forward(QKV, far)
    for which in (UP0, UP1, DOWN):
        own_shards[which].wait()
        pass_over(which, region).start()
    send_own(UP0)
    hand_on(shared_of(0), a_send, a_recv.at[0])
    fine_chunk(1)
    for far in fars[1:]:
        forward(PROJ, far)
    merge_chunk(1)
    gather(shared_of(1), a_send, a_recv.at[1])
    send_own(UP1)
    collect(QKV, fars)
    take_over(QKV)

    at_key = lax.broadcasted_iota(jnp.int32, (cells, cells), 0)
    block_cells = WIN // group
    inside = len(near) * block_cells
    place = jnp.where(
        at_key < inside, at_key + block_cells, jnp.where(at_key < inside + block_cells, at_key - inside, at_key)
    )

    heads_here = g_qkv.shape[1] // (3 * HD)

    def coarse_attention(ks):
        packed_of = [
            jnp.concatenate(
                [dot(shared[index, plane[k][1]], g_qkv[...]) for index in range(2)], axis=0
            ).astype(BF16)
            for k in ks
        ]
        for k, its in zip(ks, packed_of):
            parts_of = attend(its, heads_here, place < counts[plane[k][1]])
            if k == 0:
                got_blend[head] = jnp.concatenate(parts_of, axis=1)
            else:
                sent_blend[k] = jnp.concatenate(parts_of, axis=1)

    forward(UP0, 1)
    coarse_attention([0])
    hand_on(shared_of(1), a_send, a_recv.at[1])
    collect(PROJ, fars[1:])
    for s in range(2, chips):
        spread_proj(s)
    forward(UP1, 1)
    for far in fars[1:]:
        forward(UP0, far)
    send_own(DOWN)
    for ks in [range(1, min(3, head_count)), range(3, head_count)]:
        for k in ks:
            for index in range(2):
                arrived(shared_of(index), k, a_recv.at[index])
        coarse_attention(ks)
        for k in ks:
            remote(sent_blend.at[k], got_blend.at[head], b_send, b_recv, plane[k]).start()
        if 1 in ks:
            for far in fars[1:]:
                forward(UP1, far)
    forward(DOWN, 1)
    others = pl.ds(0, head_count - 1)
    received(g_proj.at[others, pl.ds(0, chips)], q_recv)
    for s in range(chips):
        owner = chip_at(s) * 2 + core
        for k in range(1, head_count):
            piece = g_proj.at[plane[k][1], owner]
            remote(piece, piece, x_send, x_recv, partner).start()
    take_over(PROJ)
    received(g_proj.at[others, pl.ds(0, chips)], x_recv)
    received(got_blend.at[others], b_recv)
    for r in range(region_count):
        w = g_proj.shape[3]
        total_of = dot(got_blend[0], g_proj[0, r])
        for h in range(1, head_count):
            total_of += dot(got_blend[h], g_proj[h, r])
        mid[:, r * w : (r + 1) * w] = coarse[:, r * w : (r + 1) * w] + total_of

    def row_block(h):
        return pl.ds(pl.multiple_of(h * cells, cells), cells)

    def normed_of(h):
        return c_normed.at[row_block(h)]

    c_normed[row_block(head), :] = norm(mid[...]).astype(BF16)
    gather(normed_of, m_send, m_recv)
    for far in fars[1:]:
        forward(DOWN, far)
    own[5].wait()
    own[6].wait()
    for c in range(C // 256):
        at = slice(c * 256, (c + 1) * 256)
        fine[:, at] = dot(fine_bf[...], v_out[:C, at])
    hand_on(normed_of, m_send, m_recv)
    for which in (UP0, UP1):
        collect(which, fars)
        take_over(which)
    w = g_down.shape[2]
    pair = 2 * w

    def columns_of(s):
        return pl.ds(pl.multiple_of(chip_at(s) * pair, pair), pair)

    def down_ready(s):
        holder = chip_at(s)
        if s > 0:
            for far in fars:
                for way in ways:
                    @pl.when(came(way, far) & jnp.logical_not(goes(way)) & (owner_of(way, far) // 2 == holder))
                    def _():
                        arrive(DOWN, way, far, False)
        received(slot(DOWN, holder * 2 + 1 - core), p_recv.at[DOWN + holder])

    def down(k, s):
        holder = chip_at(s)
        weights = jnp.concatenate([g_down[holder * 2], g_down[holder * 2 + 1]], axis=1)
        product = dot(c_hidden[row_block(plane[k][1]), :], weights)
        if k == 0:
            mid[:, columns_of(s)] += product
        else:
            parts[k, :, columns_of(s)] = product.astype(BF16)

    def send_back(k, s):
        remote(parts.at[k, :, columns_of(s)], got_parts.at[k - 1, :, columns_of(s)],
               r_send, r_recv.at[s], plane[k]).start()

    early = min(2, chips)
    for k in range(head_count):
        at = row_block(plane[k][1])
        if k > 0:
            arrived(normed_of, k, m_recv)
        c_hidden[at, :] = gelu(dot(c_normed[at, :], g_up[...])).astype(BF16)
        for s in range(early):
            if k == 0:
                down_ready(s)
        for s in range(early):
            down(k, s)
            if k > 0:
                send_back(k, s)
    for s in range(early, chips):
        down_ready(s)
        for k in [*range(1, head_count), 0]:
            down(k, s)
            if k > 0:
                send_back(k, s)
    for s in range(chips):
        columns = columns_of(s)
        received(got_parts.at[others, :, columns], r_recv.at[s])
        result = mid[:, columns]
        for k in range(1, head_count):
            result += got_parts[k - 1, :, columns].astype(F32)
        result = result.astype(BF16)
        for k in range(group):
            at = slice(k * C, (k + 1) * C)
            piece = dot(result, v_expand[columns, at])
            if s > 0:
                piece += wide[:, at]
            wide[:, at] = piece
    for first, last in spans:
        low, high = first // group, last // group
        spread[first:last, :] = jnp.concatenate(
            [wide[low:high, k * C : (k + 1) * C] for k in range(group)], axis=0
        ).astype(BF16)
    for c in range(C // 128):
        at = slice(c * 128, (c + 1) * 128)
        value = fine[:, at] + dot(spread[...], v_out[C:, at])
        for first, last in spans:
            count = (last - first) // group
            for k in range(group):
                lanes[c, pl.ds(first + k, count, stride=group), :] = value[first + k * count : first + (k + 1) * count, :]
        for p, j in enumerate(order):
            out[j * WIN : (j + 1) * WIN, at] = lanes[c, p * WIN : (p + 1) * WIN, :]

    sent(extended.at[pl.ds(0, 2 * WIN)], halo_send)
    sent(shared.at[pl.ds(0, 2), others], a_send)
    sent(g_proj.at[others, pl.ds(0, chips)], q_send)
    sent(g_proj.at[others, pl.ds(0, chips)], x_send)
    sent(sent_blend.at[others], b_send)
    sent(c_normed.at[pl.ds(0, (head_count - 1) * cells)], m_send)
    sent(parts.at[others], r_send)
    for which in range(5):
        sent(stack(which, chips), p_send.at[which])
    for place in range(chips):
        hops = (place + 1) * (place < chips - 1) + (chips - place) * (place > 0)

        @pl.when(chip == place)
        def _():
            for which in range(5):
                sent(stack(which, hops), z_send.at[which])


def body(region_count, head_count, tokens, shift, counts, *weights):
    rows = tokens.shape[0]
    w_qkv, w_proj, w_up, w_down, w_merge, c_qkv, c_proj, c_up, c_down, w_expand, w_out = weights
    width = w_merge.shape[1]
    group = w_merge.shape[0] // C
    cells = rows // group
    vmem = pltpu.VMEM
    dma = pltpu.SemaphoreType.DMA
    chips = region_count // 2
    mine = c_proj.shape[0]
    scratch = [vmem(tokens.shape, F32)]
    scratch += [vmem(w.shape, BF16) for w in (w_qkv, w_proj, w_up, w_down, w_merge, w_expand, w_out)]
    scratch += [
        vmem((width, c_qkv.shape[1]), BF16),
        vmem((head_count, region_count) + c_proj.shape, BF16),
        vmem((width, c_up.shape[1]), BF16),
        vmem((region_count,) + c_down.shape, BF16),
        vmem((rows + 2 * WIN, C), BF16),
        vmem((rows + WIN, C), BF16),
        vmem((rows + WIN, w_qkv.shape[1]), BF16),
        vmem((rows + WIN, C), BF16),
        vmem((rows, C), F32),
        vmem((rows, C), BF16),
        vmem((rows, w_up.shape[1]), BF16),
        vmem((cells, width), F32),
        vmem((2, head_count, cells // 2, width), BF16),
        vmem((head_count, cells, mine), BF16),
        vmem((head_count, cells, mine), BF16),
        vmem((cells, width), F32),
        vmem((head_count * cells, width), BF16),
        vmem((head_count * cells, c_up.shape[1]), BF16),
        vmem((head_count, cells, width), BF16),
        vmem((head_count, cells, width), BF16),
        vmem((cells, group * C), F32),
        vmem((rows, C), BF16),
        vmem((C // 128, rows, 128), F32),
        dma((8,)), dma, dma, dma((5,)), dma((5,)), dma((5, chips)), dma((5,)), dma((4 + chips,)), dma, dma, dma, dma,
        dma, dma((2, max(head_count, 4))), dma, dma, dma, dma((max(head_count, 4),)), dma, dma((chips,)),
    ]
    placed = [pltpu.with_memory_space_constraint(w, pltpu.HBM) for w in (tokens,) + weights]
    return pl.pallas_call(
        functools.partial(kernel, region_count, head_count),
        out_shape=jax.ShapeDtypeStruct((rows, C), F32),
        in_specs=[pl.BlockSpec(memory_space=pltpu.SMEM)] * 2
        + [pl.BlockSpec(memory_space=pltpu.HBM)] * len(placed),
        out_specs=pl.BlockSpec(memory_space=pltpu.VMEM),
        scratch_shapes=scratch,
        compiler_params=pltpu.CompilerParams(
            collective_id=0, has_side_effects=True, vmem_limit_bytes=50 * 1024 * 1024
        ),
    )(shift, pltpu.with_memory_space_constraint(counts, pltpu.HBM), *placed)


def solution(mesh):
    in_specs = (
        P(("region", "head"), None), P(), P("region"), P(), P(), P(), P(), P(),
        P("region", "head"), P("head", "region"), P("region", "head"), P("head", "region"), P(), P(),
    )
    out_specs = P(("region", "head"), None)
    run = functools.partial(body, mesh.shape["region"], mesh.shape["head"])
    return jax.shard_map(run, mesh=mesh, in_specs=in_specs, out_specs=out_specs, check_vma=False)
```

```python
import functools

import jax
import jax.numpy as jnp
from jax import lax
from jax.experimental import pallas as pl
from jax.experimental.pallas import tpu as pltpu
from jax.sharding import PartitionSpec as P

C = 512
HD = 64
HF = 8
WIN = 144
HEADS = HF
MESH = pl.DeviceIdType.MESH
F32 = jnp.float32
BF16 = jnp.bfloat16
LOG2E = 1.4426950408889634


def norm(values):
    average = jnp.mean(values, axis=-1, keepdims=True)
    centred = values - average
    spread = jnp.mean(centred * centred, axis=-1, keepdims=True)
    return centred * lax.rsqrt(spread + 1e-05)


def gelu(values):
    return 0.5 * values * (1.0 + lax.erf(values * (0.5**0.5)))


def dot(left, right):
    return jnp.dot(left, right, preferred_element_type=F32)


def flip(index, mask):
    result = index
    bit = 1
    while bit <= mask:
        if mask & bit:
            result = result + (1 - 2 * ((index // bit) % 2)) * bit
        bit *= 2
    return result


def attend(packed, head_count, visible):
    scale = HD**-0.5
    blended = []
    for head in range(head_count):
        base = head * 3 * HD
        query = packed[:, base : base + HD]
        key = packed[:, base + HD : base + 2 * HD]
        value = packed[:, base + 2 * HD : base + 3 * HD]
        scores = lax.dot_general(
            key, query, (((1,), (1,)), ((), ())), preferred_element_type=F32
        )
        if visible is not None:
            scores = jnp.where(visible, scores, -1e30 / scale)
        raised = jnp.exp2((scores - jnp.max(scores, axis=0, keepdims=True)) * (scale * LOG2E))
        weights = (raised * (1.0 / jnp.sum(raised, axis=0, keepdims=True))).astype(BF16)
        mixed = lax.dot_general(
            weights, value, (((0,), (0,)), ((), ())), preferred_element_type=F32
        )
        blended.append(mixed.astype(BF16))
    return blended


def kernel(
    region_count, head_count,
    shift, counts, tokens_in, w_qkv, w_proj, w_up, w_down, w_merge,
    c_qkv, c_proj, c_up, c_down, w_expand, w_out,
    out,
    tokens, v_qkv, v_proj, v_up, v_down, v_merge, v_expand, v_out,
    g_qkv, g_proj, g_up, g_down,
    extended, rolled, packed, blended, fine, fine_bf, hidden,
    coarse, shared, sent_blend, got_blend, mid, c_normed, c_hidden, parts, got_parts,
    wide, spread, lanes,
    local_sem, halo_send, halo_recv, own_sem, z_send, z_recv, p_send, p_recv, q_send, q_recv, x_send, x_recv,
    a_send, a_recv, b_send, b_recv, m_send, m_recv, r_send, r_recv,
):
    region, head = lax.axis_index("region"), lax.axis_index("head")
    chips = region_count // 2
    chip, core = region // 2, region % 2
    rows = tokens.shape[0]
    blocks = rows // WIN
    flat = region * head_count + head
    total = region_count * head_count
    before, after = (flat + total - 1) % total, (flat + 1) % total
    before = (before // head_count, before % head_count)
    after = (after // head_count, after % head_count)
    partner = (chip * 2 + 1 - core, head)
    plane = [(region, flip(head, k)) for k in range(head_count)]
    ways = (1, -1)

    def line(way):
        return (((chip + way + chips) % chips) * 2 + core, head)

    barrier = pltpu.get_barrier_semaphore()
    greeted = [before, after, partner, line(1), line(-1)] + plane[1:]
    for device in greeted:
        pl.semaphore_signal(barrier, inc=1, device_id=device, device_id_type=MESH)

    PROJ, QKV0, QKV1, UP0, UP1, DOWN = range(6)
    half_qkv, half_up = c_qkv.shape[0] // 2, c_up.shape[0] // 2
    shards = [c_proj, c_qkv.at[pl.ds(0, half_qkv)], c_qkv.at[pl.ds(half_qkv, half_qkv)],
              c_up.at[pl.ds(0, half_up)], c_up.at[pl.ds(half_up, half_up)], c_down]

    def slot(which, owner):
        if which in (QKV0, QKV1):
            return g_qkv.at[pl.ds(owner * c_qkv.shape[0] + (which - QKV0) * half_qkv, half_qkv)]
        if which == PROJ:
            return g_proj.at[head, owner]
        if which == UP0:
            return g_up.at[pl.ds(owner * c_up.shape[0], half_up)]
        if which == UP1:
            return g_up.at[pl.ds(owner * c_up.shape[0] + half_up, half_up)]
        return g_down.at[owner]

    token_load = pltpu.make_async_copy(tokens_in, tokens, local_sem.at[7])
    token_load.start()

    own_shards = []
    for which in range(6):
        own_shards.append(pltpu.make_async_copy(shards[which], slot(which, region), own_sem.at[which]))
    own = []
    for at, (source, target) in enumerate(
        [(w_qkv, v_qkv), (w_proj, v_proj), (w_up, v_up), (w_down, v_down), (w_merge, v_merge),
         (w_expand, v_expand), (w_out, v_out)]
    ):
        own.append(pltpu.make_async_copy(source, target, local_sem.at[at]))
    for copy in (*own_shards[:3], own[0], own[1]):
        copy.start()

    def remote(source, target, send, recv, device):
        return pltpu.make_async_remote_copy(
            src_ref=source, dst_ref=target, send_sem=send, recv_sem=recv,
            device_id=device, device_id_type=MESH,
        )

    def received(place, sem):
        remote(place, place, sem, sem, partner).wait_recv()

    def sent(place, sem):
        remote(place, place, sem, sem, partner).wait_send()

    def stack(which, n):
        if which in (QKV0, QKV1):
            return g_qkv.at[pl.ds(0, n * half_qkv)]
        if which == PROJ:
            return g_proj.at[0, pl.ds(0, n)]
        if which == DOWN:
            return g_down.at[pl.ds(0, n)]
        return g_up.at[pl.ds(0, n * half_up)]

    token_load.wait()
    extended[WIN : WIN + rows, :] = norm(tokens[...]).astype(BF16)
    pl.semaphore_wait(barrier, len(greeted))

    halo_left = remote(extended.at[pl.ds(WIN, WIN)], extended.at[pl.ds(WIN + rows, WIN)],
                       halo_send, halo_recv, before)
    halo_right = remote(extended.at[pl.ds(rows, WIN)], extended.at[pl.ds(0, WIN)],
                        halo_send, halo_recv, after)
    halo_left.start()
    halo_right.start()

    def came(way, far):
        return (chip - way * far >= 0) & (chip - way * far < chips)

    def goes(way):
        return (chip + way >= 0) & (chip + way < chips)

    def owner_of(way, far):
        return ((chip - way * far + chips * chips) % chips) * 2 + core

    def hop(which, way, far):
        owner = owner_of(way, far)
        place = slot(which, owner)
        return remote(place, place, z_send.at[which], z_recv.at[which, owner // 2], line(way))

    def pass_over(which, owner):
        place = slot(which, owner)
        arrival = p_recv.at[which + owner // 2 if which == DOWN else which]
        return remote(place, place, p_send.at[which], arrival, partner)

    def chip_at(s):
        if chips != 4:
            return (chip + s) % chips
        side = chip // 2
        return (chip, flip(chip, 1), 2 * (1 - side) + side, 2 * (1 - side) + 1 - side)[s]

    def spread_proj(s):
        owner = chip_at(s) * 2 + core
        for k in range(1, head_count):
            piece = g_proj.at[head, owner]
            remote(piece, piece, q_send, q_recv.at[s // 2], plane[k]).start()

    def send_own(which):
        for way in ways:
            @pl.when(goes(way))
            def _():
                hop(which, way, 0).start()

    def arrive(which, way, far, forward):
        owner = owner_of(way, far)
        received(slot(which, owner), z_recv.at[which, owner // 2])
        if forward:
            hop(which, way, far).start()
        pass_over(which, owner).start()

    def forward(which, far):
        if far > chips - 2:
            return
        for way in ways:
            @pl.when(came(way, far) & goes(way))
            def _():
                arrive(which, way, far, True)

    def collect(which, fars):
        for far in fars:
            for way in ways:
                @pl.when(came(way, far) & jnp.logical_not(goes(way)))
                def _():
                    arrive(which, way, far, False)

    def take_over(which):
        received(stack(which, chips), p_recv.at[which])

    fars = range(1, chips)
    others = pl.ds(0, head_count - 1)

    def pass_proj(part):
        these = range(2 * part, min(2 * part + 2, chips))
        received(g_proj.at[others, pl.ds(0, len(these))], q_recv.at[part])
        for s in these:
            for k in range(1, head_count):
                piece = g_proj.at[plane[k][1], chip_at(s) * 2 + core]
                remote(piece, piece, x_send, x_recv, partner).start()

    for which in (PROJ, QKV0, QKV1):
        own_shards[which].wait()
        send_own(which)
        pass_over(which, region).start()
    for copy in own[2:5] + own_shards[3:] + own[5:]:
        copy.start()

    relay = head_count == 4

    def half_of(piece_of, h, i):
        whole = piece_of(h)
        half = whole.shape[1] // 2
        return whole.at[:, pl.ds(i * half, half)]

    def gather(piece_of, send, recv):
        for i in range(2):
            for k in range(1, 3 if relay else head_count):
                which = i if k != 2 else 1 - i
                piece = half_of(piece_of, head, which)
                lane = recv.at[(k - 1 if which == k - 1 else 2) if relay else k]
                remote(piece, piece, send, lane, plane[k]).start()

    def hand_on(piece_of, send, recv):
        if not relay:
            return
        for i, (came_by, goes_by) in enumerate(((1, 2), (2, 1))):
            piece = half_of(piece_of, flip(head, came_by), i)
            received(piece, recv.at[i])
            remote(piece, piece, send, recv.at[3], plane[goes_by]).start()

    def arrived(piece_of, k, recv):
        if not relay or k == 3:
            received(piece_of(flip(head, k)), recv.at[k])
        elif k == 1:
            received(piece_of(head), recv.at[2])

    offset = shift[0]
    at_row = lax.broadcasted_iota(jnp.int32, (WIN, 2 * WIN), 0)
    at_column = lax.broadcasted_iota(jnp.int32, (WIN, 2 * WIN), 1)
    forth = (at_column == at_row + offset).astype(F32).astype(BF16)
    back = (at_column == at_row + (WIN - offset)).astype(F32).astype(BF16)

    def place_of(j):
        return (j - 1) % (blocks + 1) if j > 0 else blocks - 1

    def roll_window(j):
        to = place_of(j) if j < blocks else blocks
        rolled[to * WIN : (to + 1) * WIN, :] = dot(
            forth, extended[j * WIN : (j + 2) * WIN, :]
        ).astype(BF16)

    def project_rows(first, last):
        packed[first:last, :] = dot(rolled[first:last, :], v_qkv[...]).astype(BF16)

    inner = blocks - 1

    def windows(first, last):
        for place in range(first, last):
            target = place + 1 if place < inner else (place - inner) * blocks
            at = slice(place * WIN, (place + 1) * WIN)
            blended[target * WIN : (target + 1) * WIN, :] = jnp.concatenate(
                attend(packed[at, :], HEADS, None), axis=1
            )

    group = w_merge.shape[0] // C
    cells = rows // group
    width = coarse.shape[1]
    near, edge = list(range(1, blocks - 1)), [0, blocks - 1]
    order = near + edge
    spans = [(0, len(near) * WIN), (len(near) * WIN, rows)]

    def fine_chunk(index):
        first, last = spans[index]
        members_of = (near, edge)[index]
        for p, j in enumerate(members_of):
            rolled[first + p * WIN : first + (p + 1) * WIN, :] = dot(
                back, blended[j * WIN : (j + 2) * WIN, :]
            ).astype(BF16)
        own[1].wait() if index == 0 else None
        attended = dot(rolled[first:last, :], v_proj[...])
        for p, j in enumerate(members_of):
            fine[first + p * WIN : first + (p + 1) * WIN, :] = (
                tokens[j * WIN : (j + 1) * WIN, :] + attended[p * WIN : (p + 1) * WIN, :]
            )
        rolled[first:last, :] = norm(fine[first:last, :]).astype(BF16)
        own[2].wait() if index == 0 else None
        hidden[first:last, :] = gelu(dot(rolled[first:last, :], v_up[...])).astype(BF16)
        own[3].wait() if index == 0 else None
        fine[first:last, :] += dot(hidden[first:last, :], v_down[...])

    def merge_chunk(index):
        first, last = spans[index]
        low, high = first // group, last // group
        for c in range(C // 128):
            lanes[c, first:last, :] = fine[first:last, c * 128 : (c + 1) * 128]
        members = []
        for k in range(group):
            pieces = [lanes[c, pl.ds(first + k, high - low, stride=group), :] for c in range(C // 128)]
            members.append(jnp.concatenate(pieces, axis=1))
        fine_bf[first:last, :] = jnp.concatenate(members, axis=0).astype(BF16)
        own[4].wait() if index == 0 else None
        coarse[low:high, :] = dot(norm(jnp.concatenate(members, axis=1)).astype(BF16), v_merge[...])
        shared[index, head] = norm(coarse[low:high, :]).astype(BF16)

    def shared_of(index):
        return lambda h: shared.at[index, h]

    for j in range(1, blocks):
        roll_window(j)
    own[0].wait()
    project_rows(0, inner * WIN)
    windows(0, inner)
    fine_chunk(0)
    spread_proj(0)
    forward(PROJ, 1)
    forward(QKV0, 1)
    merge_chunk(0)
    gather(shared_of(0), a_send, a_recv.at[0])
    forward(QKV1, 1)
    received(extended.at[pl.ds(0, 2 * WIN)], halo_recv)
    collect(PROJ, fars[:1])
    for far in fars[1:]:
        forward(PROJ, far)
    for which in (UP0, UP1, DOWN):
        own_shards[which].wait()
        pass_over(which, region).start()
    send_own(UP0)
    roll_window(0)
    roll_window(blocks)
    project_rows(inner * WIN, (blocks + 1) * WIN)
    windows(inner, blocks + 1)
    hand_on(shared_of(0), a_send, a_recv.at[0])
    for s in range(1, min(2, chips)):
        spread_proj(s)
    for far in fars[1:]:
        forward(QKV0, far)
    fine_chunk(1)
    for far in fars[1:]:
        forward(QKV1, far)
    send_own(UP1)
    merge_chunk(1)
    gather(shared_of(1), a_send, a_recv.at[1])
    forward(UP0, 1)
    hand_on(shared_of(1), a_send, a_recv.at[1])
    collect(PROJ, fars[1:])
    for s in range(2, chips):
        spread_proj(s)
    forward(UP1, 1)
    for which in (QKV0, QKV1):
        collect(which, fars[:2])
    for which in (QKV0, QKV1):
        collect(which, fars[2:])
    for which in (QKV0, QKV1):
        take_over(which)

    at_key = lax.broadcasted_iota(jnp.int32, (cells, cells), 0)
    block_cells = WIN // group
    inside = len(near) * block_cells
    place = jnp.where(
        at_key < inside, at_key + block_cells, jnp.where(at_key < inside + block_cells, at_key - inside, at_key)
    )

    heads_here = g_qkv.shape[1] // (3 * HD)

    def coarse_attention(ks):
        packed_of = [
            jnp.concatenate(
                [dot(shared[index, plane[k][1]], g_qkv[...]) for index in range(2)], axis=0
            ).astype(BF16)
            for k in ks
        ]
        for k, its in zip(ks, packed_of):
            parts_of = attend(its, heads_here, place < counts[plane[k][1]])
            if k == 0:
                got_blend[head] = jnp.concatenate(parts_of, axis=1)
            else:
                sent_blend[k] = jnp.concatenate(parts_of, axis=1)

    pass_proj(0)
    coarse_attention([0])
    for far in fars[1:]:
        forward(UP0, far)
    for ks in [range(1, min(3, head_count)), range(3, head_count)]:
        for k in ks:
            for index in range(2):
                arrived(shared_of(index), k, a_recv.at[index])
        coarse_attention(ks)
        for k in ks:
            remote(sent_blend.at[k], got_blend.at[head], b_send, b_recv, plane[k]).start()
        if 1 in ks:
            send_own(DOWN)
    for far in fars[1:]:
        forward(UP1, far)
    for part in range(1, (chips + 1) // 2):
        pass_proj(part)
    take_over(PROJ)
    received(g_proj.at[others, pl.ds(0, chips)], x_recv)
    received(got_blend.at[others], b_recv)
    for r in range(region_count):
        w = g_proj.shape[3]
        total_of = dot(got_blend[0], g_proj[0, r])
        for h in range(1, head_count):
            total_of += dot(got_blend[h], g_proj[h, r])
        mid[:, r * w : (r + 1) * w] = coarse[:, r * w : (r + 1) * w] + total_of

    def row_block(h):
        return pl.ds(pl.multiple_of(h * cells, cells), cells)

    def normed_of(h):
        return c_normed.at[row_block(h)]

    c_normed[row_block(head), :] = norm(mid[...]).astype(BF16)
    gather(normed_of, m_send, m_recv)
    collect(UP0, fars)
    collect(UP1, fars[:1])
    forward(DOWN, 1)
    own[5].wait()
    own[6].wait()
    for c in range(C // 256):
        at = slice(c * 256, (c + 1) * 256)
        fine[:, at] = dot(fine_bf[...], v_out[:C, at])
    hand_on(normed_of, m_send, m_recv)
    w = g_down.shape[2]
    pair = 2 * w

    def columns_of(s):
        return pl.ds(pl.multiple_of(chip_at(s) * pair, pair), pair)

    def down_collect(s):
        for far in fars:
            for way in ways:
                @pl.when(came(way, far) & jnp.logical_not(goes(way)) & (owner_of(way, far) // 2 == chip_at(s)))
                def _():
                    arrive(DOWN, way, far, False)

    def down_take(s):
        holder = chip_at(s)
        received(slot(DOWN, holder * 2 + 1 - core), p_recv.at[DOWN + holder])

    def down(k, s):
        holder = chip_at(s)
        weights = jnp.concatenate([g_down[holder * 2], g_down[holder * 2 + 1]], axis=1)
        product = dot(c_hidden[row_block(plane[k][1]), :], weights)
        if k == 0:
            mid[:, columns_of(s)] += product
        else:
            parts[k, :, columns_of(s)] = product.astype(BF16)

    def send_back(k, s):
        remote(parts.at[k, :, columns_of(s)], got_parts.at[k - 1, :, columns_of(s)],
               r_send, r_recv.at[s], plane[k]).start()

    early = min(2, chips)
    collect(UP1, fars[1:])
    for s in range(1, early):
        down_collect(s)
    for which in (UP0, UP1):
        take_over(which)
    for k in range(head_count):
        at = row_block(plane[k][1])
        if k > 0:
            arrived(normed_of, k, m_recv)
        if k == 1:
            for far in fars[1:]:
                forward(DOWN, far)
        c_hidden[at, :] = gelu(dot(c_normed[at, :], g_up[...])).astype(BF16)
        if k == 2:
            for s in range(early, min(early + 1, chips)):
                down_collect(s)
        for s in range(early):
            if k == 0:
                down_take(s)
        for s in range(early):
            down(k, s)
            if k > 0:
                send_back(k, s)
    for s in range(early, chips):
        if s > early or head_count < 3:
            down_collect(s)
        down_take(s)
        for k in [*range(1, head_count), 0]:
            down(k, s)
            if k > 0:
                send_back(k, s)
    for s in range(chips):
        columns = columns_of(s)
        received(got_parts.at[others, :, columns], r_recv.at[s])
        result = mid[:, columns]
        for k in range(1, head_count):
            result += got_parts[k - 1, :, columns].astype(F32)
        result = result.astype(BF16)
        for k in range(group):
            at = slice(k * C, (k + 1) * C)
            piece = dot(result, v_expand[columns, at])
            if s > 0:
                piece += wide[:, at]
            wide[:, at] = piece
    for first, last in spans:
        low, high = first // group, last // group
        spread[first:last, :] = jnp.concatenate(
            [wide[low:high, k * C : (k + 1) * C] for k in range(group)], axis=0
        ).astype(BF16)
    for c in range(C // 128):
        at = slice(c * 128, (c + 1) * 128)
        value = fine[:, at] + dot(spread[...], v_out[C:, at])
        for first, last in spans:
            count = (last - first) // group
            for k in range(group):
                lanes[c, pl.ds(first + k, count, stride=group), :] = value[first + k * count : first + (k + 1) * count, :]
        for p, j in enumerate(order):
            out[j * WIN : (j + 1) * WIN, at] = lanes[c, p * WIN : (p + 1) * WIN, :]

    sent(extended.at[pl.ds(0, 2 * WIN)], halo_send)
    sent(shared.at[pl.ds(0, 2), others], a_send)
    sent(g_proj.at[others, pl.ds(0, chips)], q_send)
    sent(g_proj.at[others, pl.ds(0, chips)], x_send)
    sent(sent_blend.at[others], b_send)
    sent(c_normed.at[pl.ds(0, (head_count - 1) * cells)], m_send)
    sent(parts.at[others], r_send)
    for which in range(6):
        sent(stack(which, chips), p_send.at[which])
    for place in range(chips):
        hops = (place + 1) * (place < chips - 1) + (chips - place) * (place > 0)

        @pl.when(chip == place)
        def _():
            for which in range(6):
                sent(stack(which, hops), z_send.at[which])


def body(region_count, head_count, tokens, shift, counts, *weights):
    rows = tokens.shape[0]
    w_qkv, w_proj, w_up, w_down, w_merge, c_qkv, c_proj, c_up, c_down, w_expand, w_out = weights
    width = w_merge.shape[1]
    group = w_merge.shape[0] // C
    cells = rows // group
    vmem = pltpu.VMEM
    dma = pltpu.SemaphoreType.DMA
    chips = region_count // 2
    mine = c_proj.shape[0]
    scratch = [vmem(tokens.shape, F32)]
    scratch += [vmem(w.shape, BF16) for w in (w_qkv, w_proj, w_up, w_down, w_merge, w_expand, w_out)]
    scratch += [
        vmem((width, c_qkv.shape[1]), BF16),
        vmem((head_count, region_count) + c_proj.shape, BF16),
        vmem((width, c_up.shape[1]), BF16),
        vmem((region_count,) + c_down.shape, BF16),
        vmem((rows + 2 * WIN, C), BF16),
        vmem((rows + WIN, C), BF16),
        vmem((rows + WIN, w_qkv.shape[1]), BF16),
        vmem((rows + WIN, C), BF16),
        vmem((rows, C), F32),
        vmem((rows, C), BF16),
        vmem((rows, w_up.shape[1]), BF16),
        vmem((cells, width), F32),
        vmem((2, head_count, cells // 2, width), BF16),
        vmem((head_count, cells, mine), BF16),
        vmem((head_count, cells, mine), BF16),
        vmem((cells, width), F32),
        vmem((head_count * cells, width), BF16),
        vmem((head_count * cells, c_up.shape[1]), BF16),
        vmem((head_count, cells, width), BF16),
        vmem((head_count, cells, width), BF16),
        vmem((cells, group * C), F32),
        vmem((rows, C), BF16),
        vmem((C // 128, rows, 128), F32),
        dma((8,)), dma, dma, dma((6,)), dma((6,)), dma((6, chips)), dma((6,)), dma((5 + chips,)), dma, dma(((chips + 1) // 2,)), dma, dma,
        dma, dma((2, max(head_count, 4))), dma, dma, dma, dma((max(head_count, 4),)), dma, dma((chips,)),
    ]
    placed = [pltpu.with_memory_space_constraint(w, pltpu.HBM) for w in (tokens,) + weights]
    return pl.pallas_call(
        functools.partial(kernel, region_count, head_count),
        out_shape=jax.ShapeDtypeStruct((rows, C), F32),
        in_specs=[pl.BlockSpec(memory_space=pltpu.SMEM)] * 2
        + [pl.BlockSpec(memory_space=pltpu.HBM)] * len(placed),
        out_specs=pl.BlockSpec(memory_space=pltpu.VMEM),
        scratch_shapes=scratch,
        compiler_params=pltpu.CompilerParams(
            collective_id=0, has_side_effects=True, vmem_limit_bytes=50 * 1024 * 1024
        ),
    )(shift, pltpu.with_memory_space_constraint(counts, pltpu.HBM), *placed)


def solution(mesh):
    in_specs = (
        P(("region", "head"), None), P(), P("region"), P(), P(), P(), P(), P(),
        P("region", "head"), P("head", "region"), P("region", "head"), P("head", "region"), P(), P(),
    )
    out_specs = P(("region", "head"), None)
    run = functools.partial(body, mesh.shape["region"], mesh.shape["head"])
    return jax.shard_map(run, mesh=mesh, in_specs=in_specs, out_specs=out_specs, check_vma=False)
```

```python
import functools

import jax
import jax.numpy as jnp
from jax import lax
from jax.experimental import pallas as pl
from jax.experimental.pallas import tpu as pltpu
from jax.sharding import PartitionSpec as P

C = 512
HD = 64
HF = 8
WIN = 144
HEADS = HF
MESH = pl.DeviceIdType.MESH
F32 = jnp.float32
BF16 = jnp.bfloat16
LOG2E = 1.4426950408889634


def norm(values):
    average = jnp.mean(values, axis=-1, keepdims=True)
    centred = values - average
    spread = jnp.mean(centred * centred, axis=-1, keepdims=True)
    return centred * lax.rsqrt(spread + 1e-05)


def gelu(values):
    return 0.5 * values * (1.0 + lax.erf(values * (0.5**0.5)))


def dot(left, right):
    return jnp.dot(left, right, preferred_element_type=F32)


def flip(index, mask):
    result = index
    bit = 1
    while bit <= mask:
        if mask & bit:
            result = result + (1 - 2 * ((index // bit) % 2)) * bit
        bit *= 2
    return result


def attend(packed, head_count, visible):
    scale = HD**-0.5
    blended = []
    for head in range(head_count):
        base = head * 3 * HD
        query = packed[:, base : base + HD]
        key = packed[:, base + HD : base + 2 * HD]
        value = packed[:, base + 2 * HD : base + 3 * HD]
        scores = lax.dot_general(
            key, query, (((1,), (1,)), ((), ())), preferred_element_type=F32
        )
        if visible is not None:
            scores = jnp.where(visible, scores, -1e30 / scale)
        raised = jnp.exp2((scores - jnp.max(scores, axis=0, keepdims=True)) * (scale * LOG2E))
        weights = (raised * (1.0 / jnp.sum(raised, axis=0, keepdims=True))).astype(BF16)
        mixed = lax.dot_general(
            weights, value, (((0,), (0,)), ((), ())), preferred_element_type=F32
        )
        blended.append(mixed.astype(BF16))
    return blended


def kernel(
    region_count, head_count,
    shift, counts, tokens_in, w_qkv, w_proj, w_up, w_down, w_merge,
    c_qkv, c_proj, c_up, c_down, w_expand, w_out,
    out,
    tokens, v_qkv, v_proj, v_up, v_down, v_merge, v_expand, v_out,
    g_qkv, g_proj, g_up, g_down,
    extended, rolled, packed, blended, fine, fine_bf, hidden,
    coarse, shared, c_packed, sent_blend, got_blend, mid, c_normed, c_hidden, parts, got_parts,
    wide, spread, lanes,
    local_sem, halo_send, halo_recv, own_sem, z_send, z_recv, p_send, p_recv, q_send, q_recv, x_send, x_recv,
    a_send, a_recv, b_send, b_recv, m_send, m_recv, r_send, r_recv,
):
    region, head = lax.axis_index("region"), lax.axis_index("head")
    chips = region_count // 2
    chip, core = region // 2, region % 2
    rows = tokens.shape[0]
    blocks = rows // WIN
    flat = region * head_count + head
    total = region_count * head_count
    before, after = (flat + total - 1) % total, (flat + 1) % total
    before = (before // head_count, before % head_count)
    after = (after // head_count, after % head_count)
    partner = (chip * 2 + 1 - core, head)
    plane = [(region, flip(head, k)) for k in range(head_count)]
    ways = (1, -1)

    def line(way):
        return (((chip + way + chips) % chips) * 2 + core, head)

    barrier = pltpu.get_barrier_semaphore()
    greeted = [before, after, partner, line(1), line(-1)] + plane[1:]
    for device in greeted:
        pl.semaphore_signal(barrier, inc=1, device_id=device, device_id_type=MESH)

    PROJ, QKV0, QKV1, UP0, UP1, DOWN = range(6)
    half_qkv, half_up = c_qkv.shape[0] // 2, c_up.shape[0] // 2
    shards = [c_proj, c_qkv.at[pl.ds(0, half_qkv)], c_qkv.at[pl.ds(half_qkv, half_qkv)],
              c_up.at[pl.ds(0, half_up)], c_up.at[pl.ds(half_up, half_up)], c_down]

    def slot(which, owner):
        if which in (QKV0, QKV1):
            return g_qkv.at[pl.ds(owner * c_qkv.shape[0] + (which - QKV0) * half_qkv, half_qkv)]
        if which == PROJ:
            return g_proj.at[head, owner]
        if which == UP0:
            return g_up.at[pl.ds(owner * c_up.shape[0], half_up)]
        if which == UP1:
            return g_up.at[pl.ds(owner * c_up.shape[0] + half_up, half_up)]
        return g_down.at[owner]

    token_load = pltpu.make_async_copy(tokens_in, tokens, local_sem.at[7])
    token_load.start()

    own_shards = []
    for which in range(6):
        own_shards.append(pltpu.make_async_copy(shards[which], slot(which, region), own_sem.at[which]))
    own = []
    for at, (source, target) in enumerate(
        [(w_qkv, v_qkv), (w_proj, v_proj), (w_up, v_up), (w_down, v_down), (w_merge, v_merge),
         (w_expand, v_expand), (w_out, v_out)]
    ):
        own.append(pltpu.make_async_copy(source, target, local_sem.at[at]))
    for copy in (*own_shards[:3], own[0], own[1]):
        copy.start()

    def remote(source, target, send, recv, device):
        return pltpu.make_async_remote_copy(
            src_ref=source, dst_ref=target, send_sem=send, recv_sem=recv,
            device_id=device, device_id_type=MESH,
        )

    def received(place, sem):
        remote(place, place, sem, sem, partner).wait_recv()

    def sent(place, sem):
        remote(place, place, sem, sem, partner).wait_send()

    def stack(which, n):
        if which in (QKV0, QKV1):
            return g_qkv.at[pl.ds(0, n * half_qkv)]
        if which == PROJ:
            return g_proj.at[0, pl.ds(0, n)]
        if which == DOWN:
            return g_down.at[pl.ds(0, n)]
        return g_up.at[pl.ds(0, n * half_up)]

    token_load.wait()
    extended[WIN : WIN + rows, :] = norm(tokens[...]).astype(BF16)
    pl.semaphore_wait(barrier, len(greeted))

    halo_left = remote(extended.at[pl.ds(WIN, WIN)], extended.at[pl.ds(WIN + rows, WIN)],
                       halo_send, halo_recv, before)
    halo_right = remote(extended.at[pl.ds(rows, WIN)], extended.at[pl.ds(0, WIN)],
                        halo_send, halo_recv, after)
    halo_left.start()
    halo_right.start()

    def came(way, far):
        return (chip - way * far >= 0) & (chip - way * far < chips)

    def goes(way):
        return (chip + way >= 0) & (chip + way < chips)

    def owner_of(way, far):
        return ((chip - way * far + chips * chips) % chips) * 2 + core

    def hop(which, way, far):
        owner = owner_of(way, far)
        place = slot(which, owner)
        return remote(place, place, z_send.at[which], z_recv.at[which, owner // 2], line(way))

    def pass_over(which, owner):
        place = slot(which, owner)
        arrival = p_recv.at[which + owner // 2 if which == DOWN else which]
        return remote(place, place, p_send.at[which], arrival, partner)

    def chip_at(s):
        if chips != 4:
            return (chip + s) % chips
        side = chip // 2
        return (chip, flip(chip, 1), 2 * (1 - side) + side, 2 * (1 - side) + 1 - side)[s]

    def spread_proj(s):
        owner = chip_at(s) * 2 + core
        for k in range(1, head_count):
            piece = g_proj.at[head, owner]
            remote(piece, piece, q_send, q_recv.at[s // 2], plane[k]).start()

    def send_own(which):
        for way in ways:
            @pl.when(goes(way))
            def _():
                hop(which, way, 0).start()

    def arrive(which, way, far, forward):
        owner = owner_of(way, far)
        received(slot(which, owner), z_recv.at[which, owner // 2])
        if forward:
            hop(which, way, far).start()
        pass_over(which, owner).start()

    def forward(which, far):
        if far > chips - 2:
            return
        for way in ways:
            @pl.when(came(way, far) & goes(way))
            def _():
                arrive(which, way, far, True)

    def collect(which, fars):
        for far in fars:
            for way in ways:
                @pl.when(came(way, far) & jnp.logical_not(goes(way)))
                def _():
                    arrive(which, way, far, False)

    def take_over(which):
        received(stack(which, chips), p_recv.at[which])

    fars = range(1, chips)
    others = pl.ds(0, head_count - 1)

    def pass_proj(part):
        these = range(2 * part, min(2 * part + 2, chips))
        received(g_proj.at[others, pl.ds(0, len(these))], q_recv.at[part])
        for s in these:
            for k in range(1, head_count):
                piece = g_proj.at[plane[k][1], chip_at(s) * 2 + core]
                remote(piece, piece, x_send, x_recv, partner).start()

    for which in (PROJ, QKV0, QKV1):
        own_shards[which].wait()
        send_own(which)
        pass_over(which, region).start()
    for copy in own[2:5] + own_shards[3:] + own[5:]:
        copy.start()

    relay = head_count == 4

    def half_of(piece_of, h, i):
        whole = piece_of(h)
        half = whole.shape[1] // 2
        return whole.at[:, pl.ds(i * half, half)]

    def gather(piece_of, send, recv):
        for i in range(2):
            for k in range(1, 3 if relay else head_count):
                which = i if k != 2 else 1 - i
                piece = half_of(piece_of, head, which)
                lane = recv.at[(k - 1 if which == k - 1 else 2) if relay else k]
                remote(piece, piece, send, lane, plane[k]).start()

    def hand_on(piece_of, send, recv):
        if not relay:
            return
        for i, (came_by, goes_by) in enumerate(((1, 2), (2, 1))):
            piece = half_of(piece_of, flip(head, came_by), i)
            received(piece, recv.at[i])
            remote(piece, piece, send, recv.at[3], plane[goes_by]).start()

    def arrived(piece_of, k, recv):
        if not relay or k == 3:
            received(piece_of(flip(head, k)), recv.at[k])
        elif k == 1:
            received(piece_of(head), recv.at[2])

    offset = shift[0]
    at_row = lax.broadcasted_iota(jnp.int32, (WIN, 2 * WIN), 0)
    at_column = lax.broadcasted_iota(jnp.int32, (WIN, 2 * WIN), 1)
    forth = (at_column == at_row + offset).astype(F32).astype(BF16)
    back = (at_column == at_row + (WIN - offset)).astype(F32).astype(BF16)

    def place_of(j):
        return (j - 1) % (blocks + 1) if j > 0 else blocks - 1

    def roll_window(j):
        to = place_of(j) if j < blocks else blocks
        rolled[to * WIN : (to + 1) * WIN, :] = dot(
            forth, extended[j * WIN : (j + 2) * WIN, :]
        ).astype(BF16)

    def project_rows(first, last):
        packed[first:last, :] = dot(rolled[first:last, :], v_qkv[...]).astype(BF16)

    inner = blocks - 1

    def windows(first, last):
        for place in range(first, last):
            target = place + 1 if place < inner else (place - inner) * blocks
            at = slice(place * WIN, (place + 1) * WIN)
            blended[target * WIN : (target + 1) * WIN, :] = jnp.concatenate(
                attend(packed[at, :], HEADS, None), axis=1
            )

    group = w_merge.shape[0] // C
    cells = rows // group
    width = coarse.shape[1]
    near, edge = list(range(1, blocks - 1)), [0, blocks - 1]
    order = near + edge
    spans = [(0, len(near) * WIN), (len(near) * WIN, rows)]

    def fine_chunk(index):
        first, last = spans[index]
        members_of = (near, edge)[index]
        for p, j in enumerate(members_of):
            rolled[first + p * WIN : first + (p + 1) * WIN, :] = dot(
                back, blended[j * WIN : (j + 2) * WIN, :]
            ).astype(BF16)
        own[1].wait() if index == 0 else None
        attended = dot(rolled[first:last, :], v_proj[...])
        for p, j in enumerate(members_of):
            fine[first + p * WIN : first + (p + 1) * WIN, :] = (
                tokens[j * WIN : (j + 1) * WIN, :] + attended[p * WIN : (p + 1) * WIN, :]
            )
        rolled[first:last, :] = norm(fine[first:last, :]).astype(BF16)
        own[2].wait() if index == 0 else None
        hidden[first:last, :] = gelu(dot(rolled[first:last, :], v_up[...])).astype(BF16)
        own[3].wait() if index == 0 else None
        fine[first:last, :] += dot(hidden[first:last, :], v_down[...])

    def merge_chunk(index):
        first, last = spans[index]
        low, high = first // group, last // group
        for c in range(C // 128):
            lanes[c, first:last, :] = fine[first:last, c * 128 : (c + 1) * 128]
        members = []
        for k in range(group):
            pieces = [lanes[c, pl.ds(first + k, high - low, stride=group), :] for c in range(C // 128)]
            members.append(jnp.concatenate(pieces, axis=1))
        fine_bf[first:last, :] = jnp.concatenate(members, axis=0).astype(BF16)
        own[4].wait() if index == 0 else None
        coarse[low:high, :] = dot(norm(jnp.concatenate(members, axis=1)).astype(BF16), v_merge[...])
        shared[index, head] = norm(coarse[low:high, :]).astype(BF16)

    def shared_of(index):
        return lambda h: shared.at[index, h]

    for j in range(1, blocks):
        roll_window(j)
    own[0].wait()
    project_rows(0, inner * WIN)
    windows(0, inner)
    fine_chunk(0)
    spread_proj(0)
    forward(PROJ, 1)
    forward(QKV0, 1)
    merge_chunk(0)
    gather(shared_of(0), a_send, a_recv.at[0])
    forward(QKV1, 1)
    received(extended.at[pl.ds(0, 2 * WIN)], halo_recv)
    collect(PROJ, fars[:1])
    for far in fars[1:]:
        forward(PROJ, far)
    for which in (UP0, UP1, DOWN):
        own_shards[which].wait()
        pass_over(which, region).start()
    send_own(UP0)
    roll_window(0)
    roll_window(blocks)
    project_rows(inner * WIN, (blocks + 1) * WIN)
    windows(inner, blocks + 1)
    hand_on(shared_of(0), a_send, a_recv.at[0])
    for s in range(1, min(2, chips)):
        spread_proj(s)
    for far in fars[1:]:
        forward(QKV0, far)
    fine_chunk(1)
    for far in fars[1:]:
        forward(QKV1, far)
    send_own(UP1)
    merge_chunk(1)
    gather(shared_of(1), a_send, a_recv.at[1])
    forward(UP0, 1)
    hand_on(shared_of(1), a_send, a_recv.at[1])
    collect(PROJ, fars[1:])
    for s in range(2, chips):
        spread_proj(s)
    forward(UP1, 1)
    for which in (QKV0, QKV1):
        collect(which, fars[:2])
    for which in (QKV0, QKV1):
        collect(which, fars[2:])
    for which in (QKV0, QKV1):
        take_over(which)

    at_key = lax.broadcasted_iota(jnp.int32, (cells, cells), 0)
    block_cells = WIN // group
    inside = len(near) * block_cells
    place = jnp.where(
        at_key < inside, at_key + block_cells, jnp.where(at_key < inside + block_cells, at_key - inside, at_key)
    )

    heads_here = g_qkv.shape[1] // (3 * HD)

    pass_proj(0)
    for far in fars[1:]:
        forward(UP0, far)
    for k in range(1, head_count):
        for index in range(2):
            arrived(shared_of(index), k, a_recv.at[index])
    gathered = jnp.concatenate(
        [shared[index, plane[k][1]] for k in range(head_count) for index in range(2)], axis=0
    )
    c_packed[...] = dot(gathered, g_qkv[...]).astype(BF16)
    for k in range(head_count):
        parts_of = attend(c_packed[k * cells : (k + 1) * cells, :], heads_here, place < counts[plane[k][1]])
        sent_blend[k] = jnp.concatenate(parts_of, axis=1)
    for k in range(head_count - 1, 0, -1):
        remote(sent_blend.at[k], got_blend.at[head], b_send, b_recv, plane[k]).start()
    got_blend[head] = sent_blend[0]
    send_own(DOWN)
    for far in fars[1:]:
        forward(UP1, far)
    for part in range(1, (chips + 1) // 2):
        pass_proj(part)
    take_over(PROJ)
    received(g_proj.at[others, pl.ds(0, chips)], x_recv)
    forward(DOWN, 1)
    received(got_blend.at[others], b_recv)
    for r in range(region_count):
        w = g_proj.shape[3]
        total_of = dot(got_blend[0], g_proj[0, r])
        for h in range(1, head_count):
            total_of += dot(got_blend[h], g_proj[h, r])
        mid[:, r * w : (r + 1) * w] = coarse[:, r * w : (r + 1) * w] + total_of

    def row_block(h):
        return pl.ds(pl.multiple_of(h * cells, cells), cells)

    def normed_of(h):
        return c_normed.at[row_block(h)]

    c_normed[row_block(head), :] = norm(mid[...]).astype(BF16)
    gather(normed_of, m_send, m_recv)
    collect(UP0, fars)
    collect(UP1, fars[:1])
    own[5].wait()
    own[6].wait()
    for c in range(C // 256):
        at = slice(c * 256, (c + 1) * 256)
        fine[:, at] = dot(fine_bf[...], v_out[:C, at])
    def down_collect(s):
        for far in fars:
            for way in ways:
                @pl.when(came(way, far) & jnp.logical_not(goes(way)) & (owner_of(way, far) // 2 == chip_at(s)))
                def _():
                    arrive(DOWN, way, far, False)

    collect(UP1, fars[1:])
    for s in range(1, min(2, chips)):
        down_collect(s)
    hand_on(normed_of, m_send, m_recv)
    w = g_down.shape[2]
    pair = 2 * w

    def columns_of(s):
        return pl.ds(pl.multiple_of(chip_at(s) * pair, pair), pair)

    def down_take(s):
        holder = chip_at(s)
        received(slot(DOWN, holder * 2 + 1 - core), p_recv.at[DOWN + holder])

    def down(k, s):
        holder = chip_at(s)
        weights = jnp.concatenate([g_down[holder * 2], g_down[holder * 2 + 1]], axis=1)
        product = dot(c_hidden[row_block(plane[k][1]), :], weights)
        if k == 0:
            mid[:, columns_of(s)] += product
        else:
            parts[k, :, columns_of(s)] = product.astype(BF16)

    def send_back(k, s):
        remote(parts.at[k, :, columns_of(s)], got_parts.at[k - 1, :, columns_of(s)],
               r_send, r_recv.at[s], plane[k]).start()

    early = min(2, chips)
    for which in (UP0, UP1):
        take_over(which)
    for far in fars[1:]:
        forward(DOWN, far)
    for k in range(head_count):
        at = row_block(plane[k][1])
        if k > 0:
            arrived(normed_of, k, m_recv)
        c_hidden[at, :] = gelu(dot(c_normed[at, :], g_up[...])).astype(BF16)
        if k == 2:
            for s in range(early, min(early + 1, chips)):
                down_collect(s)
        for s in range(early):
            if k == 0:
                down_take(s)
        for s in range(early):
            down(k, s)
            if k > 0:
                send_back(k, s)
    for s in range(early, chips):
        if s > early or head_count < 3:
            down_collect(s)
        down_take(s)
        for k in [*range(head_count - 1, 0, -1), 0]:
            down(k, s)
            if k > 0:
                send_back(k, s)
    for s in range(chips):
        columns = columns_of(s)
        received(got_parts.at[others, :, columns], r_recv.at[s])
        result = mid[:, columns]
        for k in range(1, head_count):
            result += got_parts[k - 1, :, columns].astype(F32)
        result = result.astype(BF16)
        for k in range(group):
            at = slice(k * C, (k + 1) * C)
            piece = dot(result, v_expand[columns, at])
            if s > 0:
                piece += wide[:, at]
            wide[:, at] = piece
    for first, last in spans:
        low, high = first // group, last // group
        spread[first:last, :] = jnp.concatenate(
            [wide[low:high, k * C : (k + 1) * C] for k in range(group)], axis=0
        ).astype(BF16)
    for c in range(C // 256):
        value = fine[:, c * 256 : (c + 1) * 256] + dot(spread[...], v_out[C:, c * 256 : (c + 1) * 256])
        for lane in (2 * c, 2 * c + 1):
            half = slice((lane - 2 * c) * 128, (lane - 2 * c + 1) * 128)
            for first, last in spans:
                count = (last - first) // group
                for k in range(group):
                    lanes[lane, pl.ds(first + k, count, stride=group), :] = value[
                        first + k * count : first + (k + 1) * count, half
                    ]
            for p, j in enumerate(order):
                out[j * WIN : (j + 1) * WIN, lane * 128 : (lane + 1) * 128] = lanes[lane, p * WIN : (p + 1) * WIN, :]

    sent(extended.at[pl.ds(0, 2 * WIN)], halo_send)
    sent(shared.at[pl.ds(0, 2), others], a_send)
    sent(g_proj.at[others, pl.ds(0, chips)], q_send)
    sent(g_proj.at[others, pl.ds(0, chips)], x_send)
    sent(sent_blend.at[others], b_send)
    sent(c_normed.at[pl.ds(0, (head_count - 1) * cells)], m_send)
    sent(parts.at[others], r_send)
    for which in range(6):
        sent(stack(which, chips), p_send.at[which])
    for place in range(chips):
        hops = (place + 1) * (place < chips - 1) + (chips - place) * (place > 0)

        @pl.when(chip == place)
        def _():
            for which in range(6):
                sent(stack(which, hops), z_send.at[which])


def body(region_count, head_count, tokens, shift, counts, *weights):
    rows = tokens.shape[0]
    w_qkv, w_proj, w_up, w_down, w_merge, c_qkv, c_proj, c_up, c_down, w_expand, w_out = weights
    width = w_merge.shape[1]
    group = w_merge.shape[0] // C
    cells = rows // group
    vmem = pltpu.VMEM
    dma = pltpu.SemaphoreType.DMA
    chips = region_count // 2
    mine = c_proj.shape[0]
    scratch = [vmem(tokens.shape, F32)]
    scratch += [vmem(w.shape, BF16) for w in (w_qkv, w_proj, w_up, w_down, w_merge, w_expand, w_out)]
    scratch += [
        vmem((width, c_qkv.shape[1]), BF16),
        vmem((head_count, region_count) + c_proj.shape, BF16),
        vmem((width, c_up.shape[1]), BF16),
        vmem((region_count,) + c_down.shape, BF16),
        vmem((rows + 2 * WIN, C), BF16),
        vmem((rows + WIN, C), BF16),
        vmem((rows + WIN, w_qkv.shape[1]), BF16),
        vmem((rows + WIN, C), BF16),
        vmem((rows, C), F32),
        vmem((rows, C), BF16),
        vmem((rows, w_up.shape[1]), BF16),
        vmem((cells, width), F32),
        vmem((2, head_count, cells // 2, width), BF16),
        vmem((head_count * cells, c_qkv.shape[1]), BF16),
        vmem((head_count, cells, mine), BF16),
        vmem((head_count, cells, mine), BF16),
        vmem((cells, width), F32),
        vmem((head_count * cells, width), BF16),
        vmem((head_count * cells, c_up.shape[1]), BF16),
        vmem((head_count, cells, width), BF16),
        vmem((head_count, cells, width), BF16),
        vmem((cells, group * C), F32),
        vmem((rows, C), BF16),
        vmem((C // 128, rows, 128), F32),
        dma((8,)), dma, dma, dma((6,)), dma((6,)), dma((6, chips)), dma((6,)), dma((5 + chips,)), dma, dma(((chips + 1) // 2,)), dma, dma,
        dma, dma((2, max(head_count, 4))), dma, dma, dma, dma((max(head_count, 4),)), dma, dma((chips,)),
    ]
    placed = [pltpu.with_memory_space_constraint(w, pltpu.HBM) for w in (tokens,) + weights]
    return pl.pallas_call(
        functools.partial(kernel, region_count, head_count),
        out_shape=jax.ShapeDtypeStruct((rows, C), F32),
        in_specs=[pl.BlockSpec(memory_space=pltpu.SMEM)] * 2
        + [pl.BlockSpec(memory_space=pltpu.HBM)] * len(placed),
        out_specs=pl.BlockSpec(memory_space=pltpu.VMEM),
        scratch_shapes=scratch,
        compiler_params=pltpu.CompilerParams(
            collective_id=0, has_side_effects=True, vmem_limit_bytes=50 * 1024 * 1024
        ),
    )(shift, pltpu.with_memory_space_constraint(counts, pltpu.HBM), *placed)


def solution(mesh):
    in_specs = (
        P(("region", "head"), None), P(), P("region"), P(), P(), P(), P(), P(),
        P("region", "head"), P("head", "region"), P("region", "head"), P("head", "region"), P(), P(),
    )
    out_specs = P(("region", "head"), None)
    run = functools.partial(body, mesh.shape["region"], mesh.shape["head"])
    return jax.shard_map(run, mesh=mesh, in_specs=in_specs, out_specs=out_specs, check_vma=False)
```

```python
import functools

import jax
import jax.numpy as jnp
from jax import lax
from jax.experimental import pallas as pl
from jax.experimental.pallas import tpu as pltpu
from jax.sharding import PartitionSpec as P

C = 512
HD = 64
HF = 8
WIN = 144
HEADS = HF
MESH = pl.DeviceIdType.MESH
F32 = jnp.float32
BF16 = jnp.bfloat16
LOG2E = 1.4426950408889634


def norm(values):
    average = jnp.mean(values, axis=-1, keepdims=True)
    centred = values - average
    spread = jnp.mean(centred * centred, axis=-1, keepdims=True)
    return centred * lax.rsqrt(spread + 1e-05)


def gelu(values):
    return 0.5 * values * (1.0 + lax.erf(values * (0.5**0.5)))


def dot(left, right):
    return jnp.dot(left, right, preferred_element_type=F32)


def flip(index, mask):
    result = index
    bit = 1
    while bit <= mask:
        if mask & bit:
            result = result + (1 - 2 * ((index // bit) % 2)) * bit
        bit *= 2
    return result


def attend(packed, head_count, visible):
    scale = HD**-0.5
    blended = []
    for head in range(head_count):
        base = head * 3 * HD
        query = packed[:, base : base + HD]
        key = packed[:, base + HD : base + 2 * HD]
        value = packed[:, base + 2 * HD : base + 3 * HD]
        scores = lax.dot_general(
            key, query, (((1,), (1,)), ((), ())), preferred_element_type=F32
        )
        if visible is not None:
            scores = jnp.where(visible, scores, -1e30 / scale)
        raised = jnp.exp2((scores - jnp.max(scores, axis=0, keepdims=True)) * (scale * LOG2E))
        weights = (raised * (1.0 / jnp.sum(raised, axis=0, keepdims=True))).astype(BF16)
        mixed = lax.dot_general(
            weights, value, (((0,), (0,)), ((), ())), preferred_element_type=F32
        )
        blended.append(mixed.astype(BF16))
    return blended


def kernel(
    region_count, head_count,
    shift, counts, tokens_in, w_qkv, w_proj, w_up, w_down, w_merge,
    c_qkv, c_proj, c_up, c_down, w_expand, w_out,
    out,
    tokens, v_qkv, v_proj, v_up, v_down, v_merge, v_expand, v_out,
    g_qkv, g_proj, g_up, g_down,
    extended, rolled, packed, blended, fine, fine_bf, hidden,
    coarse, shared, c_packed, sent_blend, got_blend, mid, c_normed, c_hidden, parts, got_parts,
    wide, spread, lanes,
    local_sem, halo_send, halo_recv, own_sem, z_send, z_recv, p_send, p_recv, q_send, q_recv, x_send, x_recv,
    a_send, a_recv, b_send, b_recv, m_send, m_recv, r_send, r_recv,
):
    region, head = lax.axis_index("region"), lax.axis_index("head")
    chips = region_count // 2
    chip, core = region // 2, region % 2
    rows = tokens.shape[0]
    blocks = rows // WIN
    flat = region * head_count + head
    total = region_count * head_count
    before, after = (flat + total - 1) % total, (flat + 1) % total
    before = (before // head_count, before % head_count)
    after = (after // head_count, after % head_count)
    partner = (chip * 2 + 1 - core, head)
    plane = [(region, flip(head, k)) for k in range(head_count)]
    ways = (1, -1)

    def line(way):
        return (((chip + way + chips) % chips) * 2 + core, head)

    barrier = pltpu.get_barrier_semaphore()
    greeted = [before, after, partner] + plane[1:]
    for device in greeted:
        pl.semaphore_signal(barrier, inc=1, device_id=device, device_id_type=MESH)
    for way in ways:
        @pl.when((chip + way >= 0) & (chip + way < chips))
        def _():
            pl.semaphore_signal(barrier, inc=1, device_id=line(way), device_id_type=MESH)

    PROJ, QKV0, QKV1, UP0, UP1, DOWN = range(6)
    half_qkv, half_up = c_qkv.shape[0] // 2, c_up.shape[0] // 2
    shards = [c_proj, c_qkv.at[pl.ds(0, half_qkv)], c_qkv.at[pl.ds(half_qkv, half_qkv)],
              c_up.at[pl.ds(0, half_up)], c_up.at[pl.ds(half_up, half_up)], c_down]

    def slot(which, owner):
        if which in (QKV0, QKV1):
            return g_qkv.at[pl.ds(owner * c_qkv.shape[0] + (which - QKV0) * half_qkv, half_qkv)]
        if which == PROJ:
            return g_proj.at[head, owner]
        if which == UP0:
            return g_up.at[pl.ds(owner * c_up.shape[0], half_up)]
        if which == UP1:
            return g_up.at[pl.ds(owner * c_up.shape[0] + half_up, half_up)]
        return g_down.at[owner]

    token_load = pltpu.make_async_copy(tokens_in, tokens, local_sem.at[7])
    token_load.start()

    own_shards = []
    for which in range(6):
        own_shards.append(pltpu.make_async_copy(shards[which], slot(which, region), own_sem.at[which]))
    own = []
    for at, (source, target) in enumerate(
        [(w_qkv, v_qkv), (w_proj, v_proj), (w_up, v_up), (w_down, v_down), (w_merge, v_merge),
         (w_expand, v_expand), (w_out, v_out)]
    ):
        own.append(pltpu.make_async_copy(source, target, local_sem.at[at]))
    for copy in (*own_shards[:3], own[0], own[1]):
        copy.start()

    def remote(source, target, send, recv, device):
        return pltpu.make_async_remote_copy(
            src_ref=source, dst_ref=target, send_sem=send, recv_sem=recv,
            device_id=device, device_id_type=MESH,
        )

    def received(place, sem):
        remote(place, place, sem, sem, partner).wait_recv()

    def sent(place, sem):
        remote(place, place, sem, sem, partner).wait_send()

    def stack(which, n):
        if which in (QKV0, QKV1):
            return g_qkv.at[pl.ds(0, n * half_qkv)]
        if which == PROJ:
            return g_proj.at[0, pl.ds(0, n)]
        if which == DOWN:
            return g_down.at[pl.ds(0, n)]
        return g_up.at[pl.ds(0, n * half_up)]

    token_load.wait()
    extended[WIN : WIN + rows, :] = norm(tokens[...]).astype(BF16)
    pl.semaphore_wait(barrier, len(greeted) + 1 + (chip + chips - 1) // chips - (chip + 1) // chips)

    halo_left = remote(extended.at[pl.ds(WIN, WIN)], extended.at[pl.ds(WIN + rows, WIN)],
                       halo_send, halo_recv, before)
    halo_right = remote(extended.at[pl.ds(rows, WIN)], extended.at[pl.ds(0, WIN)],
                        halo_send, halo_recv, after)
    halo_left.start()
    halo_right.start()

    def came(way, far):
        return (chip - way * far >= 0) & (chip - way * far < chips)

    def goes(way):
        return (chip + way >= 0) & (chip + way < chips)

    def owner_of(way, far):
        return ((chip - way * far + chips * chips) % chips) * 2 + core

    def hop(which, way, far):
        owner = owner_of(way, far)
        place = slot(which, owner)
        return remote(place, place, z_send.at[which], z_recv.at[which, owner // 2], line(way))

    def pass_over(which, owner):
        place = slot(which, owner)
        arrival = p_recv.at[which + owner // 2 if which == DOWN else which]
        return remote(place, place, p_send.at[which], arrival, partner)

    def chip_at(s):
        if chips != 4:
            return (chip + s) % chips
        side = chip // 2
        return (chip, flip(chip, 1), 2 * (1 - side) + side, 2 * (1 - side) + 1 - side)[s]

    def spread_proj(s):
        owner = chip_at(s) * 2 + core
        for k in range(1, head_count):
            piece = g_proj.at[head, owner]
            remote(piece, piece, q_send, q_recv.at[s // 2], plane[k]).start()

    def send_own(which):
        for way in ways:
            @pl.when(goes(way))
            def _():
                hop(which, way, 0).start()

    def arrive(which, way, far, forward):
        owner = owner_of(way, far)
        received(slot(which, owner), z_recv.at[which, owner // 2])
        if forward:
            hop(which, way, far).start()
        pass_over(which, owner).start()

    def forward(which, far):
        if far > chips - 2:
            return
        for way in ways:
            @pl.when(came(way, far) & goes(way))
            def _():
                arrive(which, way, far, True)

    def collect(which, fars):
        for far in fars:
            for way in ways:
                @pl.when(came(way, far) & jnp.logical_not(goes(way)))
                def _():
                    arrive(which, way, far, False)

    def take_over(which):
        received(stack(which, chips), p_recv.at[which])

    fars = range(1, chips)
    others = pl.ds(0, head_count - 1)

    def pass_proj(part):
        these = range(2 * part, min(2 * part + 2, chips))
        received(g_proj.at[others, pl.ds(0, len(these))], q_recv.at[part])
        for s in these:
            for k in range(1, head_count):
                piece = g_proj.at[plane[k][1], chip_at(s) * 2 + core]
                remote(piece, piece, x_send, x_recv, partner).start()

    for which in (PROJ, QKV0, QKV1):
        own_shards[which].wait()
        send_own(which)
        pass_over(which, region).start()
    for copy in own[2:5] + own_shards[3:] + own[5:]:
        copy.start()

    relay = head_count == 4

    def half_of(piece_of, h, i):
        whole = piece_of(h)
        half = whole.shape[1] // 2
        return whole.at[:, pl.ds(i * half, half)]

    def gather(piece_of, send, recv):
        for i in range(2):
            for k in range(1, 3 if relay else head_count):
                which = i if k != 2 else 1 - i
                piece = half_of(piece_of, head, which)
                lane = recv.at[(k - 1 if which == k - 1 else 2) if relay else k]
                remote(piece, piece, send, lane, plane[k]).start()

    def hand_on(piece_of, send, recv):
        if not relay:
            return
        for i, (came_by, goes_by) in enumerate(((1, 2), (2, 1))):
            piece = half_of(piece_of, flip(head, came_by), i)
            received(piece, recv.at[i])
            remote(piece, piece, send, recv.at[3], plane[goes_by]).start()

    def arrived(piece_of, k, recv):
        if not relay or k == 3:
            received(piece_of(flip(head, k)), recv.at[k])
        elif k == 1:
            received(piece_of(head), recv.at[2])

    offset = shift[0]
    at_row = lax.broadcasted_iota(jnp.int32, (WIN, 2 * WIN), 0)
    at_column = lax.broadcasted_iota(jnp.int32, (WIN, 2 * WIN), 1)
    forth = (at_column == at_row + offset).astype(F32).astype(BF16)
    back = (at_column == at_row + (WIN - offset)).astype(F32).astype(BF16)

    def place_of(j):
        return (j - 1) % (blocks + 1) if j > 0 else blocks - 1

    def roll_window(j):
        to = place_of(j) if j < blocks else blocks
        rolled[to * WIN : (to + 1) * WIN, :] = dot(
            forth, extended[j * WIN : (j + 2) * WIN, :]
        ).astype(BF16)

    def project_rows(first, last):
        packed[first:last, :] = dot(rolled[first:last, :], v_qkv[...]).astype(BF16)

    inner = blocks - 1

    def windows(first, last):
        for place in range(first, last):
            target = place + 1 if place < inner else (place - inner) * blocks
            at = slice(place * WIN, (place + 1) * WIN)
            blended[target * WIN : (target + 1) * WIN, :] = jnp.concatenate(
                attend(packed[at, :], HEADS, None), axis=1
            )

    group = w_merge.shape[0] // C
    cells = rows // group
    width = coarse.shape[1]
    near, edge = list(range(1, blocks - 1)), [0, blocks - 1]
    order = near + edge
    spans = [(0, len(near) * WIN), (len(near) * WIN, rows)]

    def fine_chunk(index):
        first, last = spans[index]
        members_of = (near, edge)[index]
        for p, j in enumerate(members_of):
            rolled[first + p * WIN : first + (p + 1) * WIN, :] = dot(
                back, blended[j * WIN : (j + 2) * WIN, :]
            ).astype(BF16)
        own[1].wait() if index == 0 else None
        attended = dot(rolled[first:last, :], v_proj[...])
        for p, j in enumerate(members_of):
            fine[first + p * WIN : first + (p + 1) * WIN, :] = (
                tokens[j * WIN : (j + 1) * WIN, :] + attended[p * WIN : (p + 1) * WIN, :]
            )
        rolled[first:last, :] = norm(fine[first:last, :]).astype(BF16)
        own[2].wait() if index == 0 else None
        hidden[first:last, :] = gelu(dot(rolled[first:last, :], v_up[...])).astype(BF16)
        own[3].wait() if index == 0 else None
        fine[first:last, :] += dot(hidden[first:last, :], v_down[...])

    def merge_chunk(index):
        first, last = spans[index]
        low, high = first // group, last // group
        for c in range(C // 128):
            lanes[c, first:last, :] = fine[first:last, c * 128 : (c + 1) * 128]
        members = []
        for k in range(group):
            pieces = [lanes[c, pl.ds(first + k, high - low, stride=group), :] for c in range(C // 128)]
            members.append(jnp.concatenate(pieces, axis=1))
        fine_bf[first:last, :] = jnp.concatenate(members, axis=0).astype(BF16)
        own[4].wait() if index == 0 else None
        coarse[low:high, :] = dot(norm(jnp.concatenate(members, axis=1)).astype(BF16), v_merge[...])
        shared[index, head] = norm(coarse[low:high, :]).astype(BF16)

    def shared_of(index):
        return lambda h: shared.at[index, h]

    for j in range(1, blocks):
        roll_window(j)
    own[0].wait()
    project_rows(0, inner * WIN)
    windows(0, inner)
    fine_chunk(0)
    spread_proj(0)
    forward(PROJ, 1)
    forward(QKV0, 1)
    merge_chunk(0)
    gather(shared_of(0), a_send, a_recv.at[0])
    forward(QKV1, 1)
    received(extended.at[pl.ds(0, 2 * WIN)], halo_recv)
    collect(PROJ, fars[:1])
    for far in fars[1:]:
        forward(PROJ, far)
    for which in (UP0, UP1, DOWN):
        own_shards[which].wait()
        pass_over(which, region).start()
    send_own(UP0)
    roll_window(0)
    roll_window(blocks)
    project_rows(inner * WIN, (blocks + 1) * WIN)
    windows(inner, blocks + 1)
    hand_on(shared_of(0), a_send, a_recv.at[0])
    for s in range(1, min(2, chips)):
        spread_proj(s)
    for far in fars[1:]:
        forward(QKV0, far)
    fine_chunk(1)
    for far in fars[1:]:
        forward(QKV1, far)
    send_own(UP1)
    merge_chunk(1)
    gather(shared_of(1), a_send, a_recv.at[1])
    forward(UP0, 1)
    hand_on(shared_of(1), a_send, a_recv.at[1])
    collect(PROJ, fars[1:])
    for s in range(2, chips):
        spread_proj(s)
    forward(UP1, 1)
    for which in (QKV0, QKV1):
        collect(which, fars[:2])
    for which in (QKV0, QKV1):
        collect(which, fars[2:])
    for which in (QKV0, QKV1):
        take_over(which)

    at_key = lax.broadcasted_iota(jnp.int32, (cells, cells), 0)
    block_cells = WIN // group
    inside = len(near) * block_cells
    place = jnp.where(
        at_key < inside, at_key + block_cells, jnp.where(at_key < inside + block_cells, at_key - inside, at_key)
    )

    heads_here = g_qkv.shape[1] // (3 * HD)

    pass_proj(0)
    for far in fars[1:]:
        forward(UP0, far)
    for k in range(1, head_count):
        for index in range(2):
            arrived(shared_of(index), k, a_recv.at[index])
    gathered = jnp.concatenate(
        [shared[index, plane[k][1]] for k in range(head_count) for index in range(2)], axis=0
    )
    c_packed[...] = dot(gathered, g_qkv[...]).astype(BF16)
    for k in range(head_count):
        parts_of = attend(c_packed[k * cells : (k + 1) * cells, :], heads_here, place < counts[plane[k][1]])
        sent_blend[k] = jnp.concatenate(parts_of, axis=1)
    for k in range(head_count - 1, 0, -1):
        remote(sent_blend.at[k], got_blend.at[head], b_send, b_recv, plane[k]).start()
    got_blend[head] = sent_blend[0]
    send_own(DOWN)
    for far in fars[1:]:
        forward(UP1, far)
    for part in range(1, (chips + 1) // 2):
        pass_proj(part)
    take_over(PROJ)
    received(g_proj.at[others, pl.ds(0, chips)], x_recv)
    forward(DOWN, 1)
    received(got_blend.at[others], b_recv)
    for r in range(region_count):
        w = g_proj.shape[3]
        total_of = dot(got_blend[0], g_proj[0, r])
        for h in range(1, head_count):
            total_of += dot(got_blend[h], g_proj[h, r])
        mid[:, r * w : (r + 1) * w] = coarse[:, r * w : (r + 1) * w] + total_of

    def row_block(h):
        return pl.ds(pl.multiple_of(h * cells, cells), cells)

    def normed_of(h):
        return c_normed.at[row_block(h)]

    c_normed[row_block(head), :] = norm(mid[...]).astype(BF16)
    gather(normed_of, m_send, m_recv)
    collect(UP0, fars)
    collect(UP1, fars[:1])
    own[5].wait()
    own[6].wait()
    for c in range(C // 256):
        at = slice(c * 256, (c + 1) * 256)
        fine[:, at] = dot(fine_bf[...], v_out[:C, at])
    def down_collect(s):
        for far in fars:
            for way in ways:
                @pl.when(came(way, far) & jnp.logical_not(goes(way)) & (owner_of(way, far) // 2 == chip_at(s)))
                def _():
                    arrive(DOWN, way, far, False)

    collect(UP1, fars[1:])
    for s in range(1, min(2, chips)):
        down_collect(s)
    hand_on(normed_of, m_send, m_recv)
    w = g_down.shape[2]
    pair = 2 * w

    def columns_of(s):
        return pl.ds(pl.multiple_of(chip_at(s) * pair, pair), pair)

    def down_take(s):
        holder = chip_at(s)
        received(slot(DOWN, holder * 2 + 1 - core), p_recv.at[DOWN + holder])

    def down(k, s):
        holder = chip_at(s)
        weights = jnp.concatenate([g_down[holder * 2], g_down[holder * 2 + 1]], axis=1)
        product = dot(c_hidden[row_block(plane[k][1]), :], weights)
        if k == 0:
            mid[:, columns_of(s)] += product
        else:
            parts[k, :, columns_of(s)] = product.astype(BF16)

    def send_back(k, s):
        remote(parts.at[k, :, columns_of(s)], got_parts.at[k - 1, :, columns_of(s)],
               r_send, r_recv.at[s], plane[k]).start()

    early = min(2, chips)
    for which in (UP0, UP1):
        take_over(which)
    for far in fars[1:]:
        forward(DOWN, far)
    for k in range(head_count):
        at = row_block(plane[k][1])
        if k > 0:
            arrived(normed_of, k, m_recv)
        c_hidden[at, :] = gelu(dot(c_normed[at, :], g_up[...])).astype(BF16)
        if k == 2:
            for s in range(early, min(early + 1, chips)):
                down_collect(s)
        for s in range(early):
            if k == 0:
                down_take(s)
        for s in range(early):
            down(k, s)
            if k > 0:
                send_back(k, s)
    for s in range(early, chips):
        if s > early or head_count < 3:
            down_collect(s)
        down_take(s)
        for k in [*range(head_count - 1, 0, -1), 0]:
            down(k, s)
            if k > 0:
                send_back(k, s)
    for s in range(chips):
        columns = columns_of(s)
        received(got_parts.at[others, :, columns], r_recv.at[s])
        result = mid[:, columns]
        for k in range(1, head_count):
            result += got_parts[k - 1, :, columns].astype(F32)
        result = result.astype(BF16)
        for k in range(group):
            at = slice(k * C, (k + 1) * C)
            piece = dot(result, v_expand[columns, at])
            if s > 0:
                piece += wide[:, at]
            wide[:, at] = piece
    for first, last in spans:
        low, high = first // group, last // group
        spread[first:last, :] = jnp.concatenate(
            [wide[low:high, k * C : (k + 1) * C] for k in range(group)], axis=0
        ).astype(BF16)
    for c in range(C // 256):
        value = fine[:, c * 256 : (c + 1) * 256] + dot(spread[...], v_out[C:, c * 256 : (c + 1) * 256])
        for lane in (2 * c, 2 * c + 1):
            half = slice((lane - 2 * c) * 128, (lane - 2 * c + 1) * 128)
            for first, last in spans:
                count = (last - first) // group
                for k in range(group):
                    lanes[lane, pl.ds(first + k, count, stride=group), :] = value[
                        first + k * count : first + (k + 1) * count, half
                    ]
            for p, j in enumerate(order):
                out[j * WIN : (j + 1) * WIN, lane * 128 : (lane + 1) * 128] = lanes[lane, p * WIN : (p + 1) * WIN, :]

    sent(extended.at[pl.ds(0, 2 * WIN)], halo_send)
    sent(shared.at[pl.ds(0, 2), others], a_send)
    sent(g_proj.at[others, pl.ds(0, chips)], q_send)
    sent(g_proj.at[others, pl.ds(0, chips)], x_send)
    sent(sent_blend.at[others], b_send)
    sent(c_normed.at[pl.ds(0, (head_count - 1) * cells)], m_send)
    sent(parts.at[others], r_send)
    for which in range(6):
        sent(stack(which, chips), p_send.at[which])
    for place in range(chips):
        hops = (place + 1) * (place < chips - 1) + (chips - place) * (place > 0)

        @pl.when(chip == place)
        def _():
            for which in range(6):
                sent(stack(which, hops), z_send.at[which])


def body(region_count, head_count, tokens, shift, counts, *weights):
    rows = tokens.shape[0]
    w_qkv, w_proj, w_up, w_down, w_merge, c_qkv, c_proj, c_up, c_down, w_expand, w_out = weights
    width = w_merge.shape[1]
    group = w_merge.shape[0] // C
    cells = rows // group
    vmem = pltpu.VMEM
    dma = pltpu.SemaphoreType.DMA
    chips = region_count // 2
    mine = c_proj.shape[0]
    scratch = [vmem(tokens.shape, F32)]
    scratch += [vmem(w.shape, BF16) for w in (w_qkv, w_proj, w_up, w_down, w_merge, w_expand, w_out)]
    scratch += [
        vmem((width, c_qkv.shape[1]), BF16),
        vmem((head_count, region_count) + c_proj.shape, BF16),
        vmem((width, c_up.shape[1]), BF16),
        vmem((region_count,) + c_down.shape, BF16),
        vmem((rows + 2 * WIN, C), BF16),
        vmem((rows + WIN, C), BF16),
        vmem((rows + WIN, w_qkv.shape[1]), BF16),
        vmem((rows + WIN, C), BF16),
        vmem((rows, C), F32),
        vmem((rows, C), BF16),
        vmem((rows, w_up.shape[1]), BF16),
        vmem((cells, width), F32),
        vmem((2, head_count, cells // 2, width), BF16),
        vmem((head_count * cells, c_qkv.shape[1]), BF16),
        vmem((head_count, cells, mine), BF16),
        vmem((head_count, cells, mine), BF16),
        vmem((cells, width), F32),
        vmem((head_count * cells, width), BF16),
        vmem((head_count * cells, c_up.shape[1]), BF16),
        vmem((head_count, cells, width), BF16),
        vmem((head_count, cells, width), BF16),
        vmem((cells, group * C), F32),
        vmem((rows, C), BF16),
        vmem((C // 128, rows, 128), F32),
        dma((8,)), dma, dma, dma((6,)), dma((6,)), dma((6, chips)), dma((6,)), dma((5 + chips,)), dma, dma(((chips + 1) // 2,)), dma, dma,
        dma, dma((2, max(head_count, 4))), dma, dma, dma, dma((max(head_count, 4),)), dma, dma((chips,)),
    ]
    placed = [pltpu.with_memory_space_constraint(w, pltpu.HBM) for w in (tokens,) + weights]
    return pl.pallas_call(
        functools.partial(kernel, region_count, head_count),
        out_shape=jax.ShapeDtypeStruct((rows, C), F32),
        in_specs=[pl.BlockSpec(memory_space=pltpu.SMEM)] * 2
        + [pl.BlockSpec(memory_space=pltpu.HBM)] * len(placed),
        out_specs=pl.BlockSpec(memory_space=pltpu.VMEM),
        scratch_shapes=scratch,
        compiler_params=pltpu.CompilerParams(
            collective_id=0, has_side_effects=True, vmem_limit_bytes=50 * 1024 * 1024
        ),
    )(shift, pltpu.with_memory_space_constraint(counts, pltpu.HBM), *placed)


def solution(mesh):
    in_specs = (
        P(("region", "head"), None), P(), P("region"), P(), P(), P(), P(), P(),
        P("region", "head"), P("head", "region"), P("region", "head"), P("head", "region"), P(), P(),
    )
    out_specs = P(("region", "head"), None)
    run = functools.partial(body, mesh.shape["region"], mesh.shape["head"])
    return jax.shard_map(run, mesh=mesh, in_specs=in_specs, out_specs=out_specs, check_vma=False)
```
